32 devices in a mesh: ray: 4 (over z), cell: 8 (over y, x, core).
Axes of the slice: x: 2, y: 2, z: 4, core: 2. Of those that a mesh axis runs over, the one named last changes fastest.
Arguments:
- right_side: float32 [8, 8192], P(None, 'ray'), may hold values from -6 to 6
- tiles: bfloat16 [32, 32, 256, 256], P('ray', 'cell'), may hold values from -0.375 to 0.375
- pattern: int32 [32, 32], P('ray', 'cell'), may hold values from 0 to 31, as said below
- counts: int32 [32, 8], P('ray', 'cell'), may hold values from 1 to 4, as said below
Outputs:
- solution: float32 [8, 65536], P(None, 'cell')
- misfit: float32 [8], replicated
The draws below stay inside these ranges and needn't reach their ends.
Inputs may be any that keep to these rules, and one draw needn't show every extreme that they name: `pattern`: each entry indexes a block within the slot's group of 32 cell blocks; a bundle may name a block more than once. Ragged counts; some bundle has all 4 slots live in some group, and some has one.
All inputs are finite; a program needn't handle non-finite values.
Results may differ from the reference program's by a relative error of at most 0.0014.
Values may be sent and summed in bfloat16 or wider, within the bound.
A program may use at most 64 MiB of HBM per device.

```python
import jax
import jax.numpy as jnp
from jax import lax

RB = 256
CB = 256
NRHS = 8
BLK_DEV = 32
KDEV = 4
ITERS = 4
SHARDS = 8
BUNDLES = 32
BLOCKS = 256
SLOTS = 32
ROWS = 8192
CELLS = 65536


def draw_pattern(key, part):
    values = jax.random.randint(jax.random.fold_in(key, 11), (BUNDLES, SLOTS), 0, BLK_DEV)
    values = values.at[0, 0].set(0).at[0, 1].set(BLK_DEV - 1)
    return values.astype(jnp.int32)


def draw_counts(key, part):
    values = jax.random.randint(jax.random.fold_in(key, 23), (BUNDLES, SHARDS), 1, KDEV + 1)
    values = values.at[0, 0].set(KDEV).at[1, 0].set(1)
    return values.astype(jnp.int32)


def shard_levels(own_key, dims, split, least, top_value):
    loudness, own = 1.0, jax.random.fold_in(own_key, 6)
    for axis_at, blocks in split:
        steps = jnp.exp(jax.random.uniform(jax.random.fold_in(own, axis_at), (blocks,), jnp.float32, least / len(split), top_value / len(split)))
        loudness = loudness * jnp.repeat(steps, dims[axis_at] // blocks).reshape([-1 if axis == axis_at else 1 for axis in range(len(dims))])
    return loudness


def noise(key, shape, scale, reach, pieces=(), kind=jnp.bfloat16):
    values = jax.random.normal(key, shape, jnp.float32) * scale
    if len(pieces) > 0:
        values = shard_levels(key, shape, pieces, -0.22, 0.18) * values
    return jnp.clip(values, min=-reach, max=reach).astype(kind)


def setup_inputs(seed: int = 0) -> dict:
    streams_of = jax.random.split(jax.random.key(seed), 5)
    right_side = noise(streams_of[0], (NRHS, ROWS), 1.0, 6.0, ((1, 4),), jnp.float32)
    tiles = noise(streams_of[1], (BUNDLES, SLOTS, RB, CB), CB ** -0.5, 0.375, ((0, 4), (1, 8)))
    pattern = draw_pattern(jax.random.fold_in(streams_of[4], 71), 0)
    counts = draw_counts(jax.random.fold_in(streams_of[4], 71), 0)
    return dict(right_side=right_side, tiles=tiles, pattern=pattern, counts=counts)


def slot_info(pattern_row, count_row):
    slot = jnp.arange(SLOTS, dtype=jnp.int32)
    group = slot // KDEV
    live = slot % KDEV < count_row[group]
    target = (group * BLK_DEV + pattern_row).astype(jnp.int32)
    return (live, target)

def forward(tiles, pattern, counts, vector):
    nrhs = vector.shape[0]
    vblocks = vector.astype(jnp.bfloat16).reshape(nrhs, BLOCKS, CB)

    def one(args):
        tile, pattern_row, count_row = args
        live, target = slot_info(pattern_row, count_row)
        picked = vblocks[:, target].astype(jnp.float32) * live[None, :, None].astype(jnp.float32)
        return jnp.einsum('src,nsc->nr', tile.astype(jnp.float32), picked)
    out = lax.map(one, (tiles, pattern, counts))
    return jnp.transpose(out, (1, 0, 2)).reshape(nrhs, ROWS)

def adjoint(tiles, pattern, counts, vector):
    nrhs = vector.shape[0]
    ublocks = jnp.transpose(vector.astype(jnp.bfloat16).reshape(nrhs, BUNDLES, RB), (1, 0, 2))

    def one(carry, args):
        tile, pattern_row, count_row, rows = args
        live, target = slot_info(pattern_row, count_row)
        per = jnp.einsum('src,nr->snc', tile.astype(jnp.float32), rows.astype(jnp.float32))
        per = per * live[:, None, None].astype(jnp.float32)
        return (carry.at[:, target].add(jnp.transpose(per, (1, 0, 2))), None)
    start = jnp.zeros((nrhs, BLOCKS, CB), jnp.float32)
    total, _ = lax.scan(one, start, (tiles, pattern, counts, ublocks))
    return total.reshape(nrhs, CELLS)

def norm_of(vector):
    return jnp.sqrt(lax.optimization_barrier(jnp.sum(vector * vector, axis=1)) + 1e-06)

def reference(right_side, tiles, pattern, counts):
    beta = norm_of(right_side)
    u = right_side / beta[:, None]
    v = adjoint(tiles, pattern, counts, u)
    alpha = norm_of(v)
    v = v / alpha[:, None]
    w = v
    x = jnp.zeros_like(v)
    phibar = beta
    rhobar = alpha
    for step in range(ITERS):
        u = forward(tiles, pattern, counts, v) - alpha[:, None] * u
        beta = norm_of(u)
        u = u / beta[:, None]
        v = adjoint(tiles, pattern, counts, u) - beta[:, None] * v
        alpha = norm_of(v)
        v = v / alpha[:, None]
        rho = jnp.sqrt(rhobar * rhobar + beta * beta)
        cosine = rhobar / rho
        sine = beta / rho
        theta = sine * alpha
        rhobar = -cosine * alpha
        phi = cosine * phibar
        phibar = sine * phibar
        x = x + (phi / rho)[:, None] * w
        w = v - (theta / rho)[:, None] * w
    return (x, phibar)
```

```python
import functools

import jax
import jax.numpy as jnp
from jax import lax
from jax.experimental import pallas as pl
from jax.experimental.pallas import tpu as pltpu
from jax.sharding import PartitionSpec as P

BLK_DEV = 32
ITERS = 4
EPS = 1e-06
F32 = jnp.float32
BF16 = jnp.bfloat16
I16 = jnp.int16
LANES = 128
STEPS = 64.0
TOP = 32700.0


def split(value):
    hi = value.astype(BF16)
    lo = (value - hi.astype(F32)).astype(BF16)
    return hi, lo


def spread(stat, lanes):
    return jnp.concatenate([stat] * (lanes // LANES), axis=1)


def total_of(value):
    total = jnp.sum(value, axis=1, keepdims=True)
    return jnp.broadcast_to(total, (value.shape[0], LANES))


def stack(value):
    return jnp.concatenate([value[:, j:j + LANES] for j in range(0, value.shape[1], LANES)], axis=0)


def unstack(value, rows):
    return jnp.concatenate([value[j:j + rows] for j in range(0, value.shape[0], rows)], axis=1)


def range_code(top):
    top = jnp.broadcast_to(jnp.max(top, axis=1, keepdims=True), (top.shape[0], LANES))
    return jnp.ceil(jnp.log2(jnp.maximum(top, 1e-30)) * STEPS) + 1.0


def code_slab(code, lanes):
    return jnp.concatenate([code] * (lanes // LANES), axis=0).astype(jnp.int32).astype(I16)


def encode(value, code):
    share = value * spread(TOP * jnp.exp2(code * (-1.0 / STEPS)), value.shape[1])
    return stack(jnp.round(share)).astype(jnp.int32).astype(I16)


def unit(slab, rows, lanes):
    code = slab[0:rows].astype(jnp.int32).astype(F32)
    return spread(jnp.exp2(code * (1.0 / STEPS)) * (1.0 / TOP), lanes)


def decode(slab, rows):
    return unstack(slab.astype(jnp.int32).astype(F32), rows)


def flipped_bits(me, d):
    peer = me
    bit = 1
    while bit <= d:
        if d // bit % 2:
            peer = peer + bit - 2 * bit * lax.rem(me // bit, 2)
        bit *= 2
    return peer


def partners(me, n):
    if n & (n - 1) == 0:
        return [(d, flipped_bits(me, d)) for d in range(n - 1, 0, -1)]
    return [(d, lax.rem(me + d, n)) for d in range(1, n)]


def kernel(
    R, C,
    pattern_hbm, counts_hbm, rhs, tiles_hbm,
    out, mis,
    tiles, flipped, fpart, fq, u, ucat, aq, arecv, hq, vdec, vb, vsh, usq, gsq, cum, w, x,
    pattern, counts, idx, prv, lst,
    tile_sem, small_sem, fs, fr, as_, ar, ns, nr, hs, hr, gs, gr,
):
    S, B = pattern.shape
    N = rhs.shape[0]
    RB, CB = tiles.shape[2], tiles.shape[3]
    NB = BLK_DEV
    K = NB // R
    slots = B * S
    me_r = lax.axis_index("ray")
    me_c = lax.axis_index("cell")
    ray = partners(me_r, R)
    cell = partners(me_c, C)

    small = [
        pltpu.make_async_copy(pattern_hbm, pattern, small_sem.at[0]),
        pltpu.make_async_copy(counts_hbm, counts, small_sem.at[1]),
    ]
    for copy in small:
        copy.start()
    loads = []
    for b in range(B):
        load = pltpu.make_async_copy(tiles_hbm.at[b], tiles.at[b], tile_sem.at[b])
        load.start()
        loads.append(load)

    barrier = pltpu.get_barrier_semaphore()
    for axis, others in (("cell", cell), ("ray", ray)):
        for _, peer in others:
            pl.semaphore_signal(barrier, inc=1, device_id={axis: peer}, device_id_type=pl.DeviceIdType.MESH)

    def remote(src, dst, send, recv, axis, peer):
        return pltpu.make_async_remote_copy(
            src_ref=src, dst_ref=dst, send_sem=send, recv_sem=recv,
            device_id={axis: peer}, device_id_type=pl.DeviceIdType.MESH,
        )

    cum[slots] = jnp.zeros((N, CB), F32)
    vb[NB] = jnp.zeros((N, CB), BF16)
    w[...] = jnp.zeros_like(w)
    x[...] = jnp.zeros_like(x)
    vsh[...] = jnp.zeros_like(vsh)
    for b in range(B):
        value = rhs[:, b * RB:(b + 1) * RB]
        u[b] = value
        hi, lo = split(value)
        ucat[b, 0:N] = hi
        ucat[b, N:2 * N] = lo

    for copy in small:
        copy.wait()
    for b in range(B):
        for s in range(S):
            idx[b * S + s] = jnp.where(s < counts[0, b], pattern[s, b], NB)

    def chain(i, carry):
        p = idx[i]
        before = jnp.int32(slots)
        last = jnp.int32(slots)
        for j in range(slots):
            q = idx[j]
            before = jnp.where((q == p) & (j < i), j, before)
            last = jnp.where(q == i, j, last)
        prv[i] = before
        lst[i] = last
        return carry

    def final(k, carry):
        last = jnp.int32(slots)
        for j in range(slots):
            last = jnp.where(idx[j] == k, j, last)
        lst[k] = last
        return carry

    assert slots <= NB
    lax.fori_loop(0, slots, chain, 0)
    lax.fori_loop(slots, NB, final, 0)

    def ray_copies(ref, send, recv):
        return [remote(ref.at[me_r], ref.at[me_r], send.at[d], recv.at[d], "ray", peer) for d, peer in ray]

    def cell_copies(ref, send, recv):
        return [remote(ref.at[me_c], ref.at[me_c], send.at[d], recv.at[d], "cell", peer) for d, peer in cell]

    def scatter_copies():
        return [remote(aq.at[peer], arecv.at[d], as_.at[d], ar.at[d], "ray", peer) for d, peer in ray]

    def start(copies):
        for copy in copies:
            copy.start()

    def finish(copies):
        for copy in copies:
            copy.wait()

    def norm_start():
        sq = jnp.zeros((N, RB), F32)
        for b in range(B):
            sq = sq + u[b] * u[b]
        usq[me_r] = total_of(sq)
        start(ray_copies(usq, ns, nr))

    def norm_end():
        finish(ray_copies(usq, ns, nr))
        total = usq[0]
        for r in range(1, R):
            total = total + usq[r]
        return jnp.sqrt(total + EPS)

    def adjoint(wait):
        for b in range(B):
            if wait:
                loads[b].wait()
            rows = ucat[b]
            for s in range(S):
                i = b * S + s
                per = lax.dot_general(rows, tiles[b, s], (((1,), (0,)), ((), ())), preferred_element_type=F32)
                cum[i] = per[0:N] + per[N:2 * N] + cum[prv[i]]
        top = jnp.zeros((N, CB), F32)
        for k in range(NB):
            top = jnp.maximum(top, jnp.abs(cum[lst[k]]))
        code = range_code(top)
        slab = code_slab(code, CB)
        for r in range(R):
            for k in range(K):
                aq[r, k] = encode(cum[lst[r * K + k]], code)
            aq[r, K] = slab

    def gather(beta, alpha, beside):
        inv = spread(1.0 / beta, CB)
        back = spread(beta / alpha, CB)
        for copy in scatter_copies():
            copy.wait_recv()
        units = {d: unit(arecv[d, K], N, CB) for d, _ in ray}
        top = jnp.zeros((N, CB), F32)
        for k in range(K):
            total = cum[lst[me_r * K + k]]
            for d, _ in ray:
                total = total + decode(arecv[d, k], N) * units[d]
            v = total * inv - back * vsh[k]
            vsh[k] = v
            top = jnp.maximum(top, jnp.abs(v))
        code = range_code(top)
        hq[me_r, K] = code_slab(code, CB)
        for k in range(K):
            hq[me_r, k] = encode(vsh[k], code)
        start(ray_copies(hq, hs, hr))
        for copy in scatter_copies():
            copy.wait_send()
        beside()

    def forward(beta, side):
        finish(ray_copies(hq, hs, hr))
        sq = jnp.zeros((N, CB), F32)
        for r in range(R):
            grain = unit(hq[r, K], N, CB)
            for k in range(K):
                v = decode(hq[r, k], N) * grain
                vdec[r * K + k] = v
                vb[r * K + k] = v.astype(BF16)
                sq = sq + v * v
        gsq[side, me_c] = total_of(sq)
        start(cell_copies(gsq.at[side], gs.at[side], gr.at[side]))
        top = jnp.zeros((N, RB), F32)
        for b in range(B):
            acc = jnp.zeros((N, RB), F32)
            for s in range(S):
                acc = acc + lax.dot_general(
                    vb[idx[b * S + s]], flipped[b, s], (((1,), (0,)), ((), ())), preferred_element_type=F32
                )
            fpart[b] = acc
            top = jnp.maximum(top, jnp.abs(acc))
        code = range_code(top)
        fq[side, me_c, B] = code_slab(code, RB)
        for b in range(B):
            fq[side, me_c, b] = encode(fpart[b], code)
        start(cell_copies(fq.at[side], fs.at[side], fr.at[side]))
        finish(cell_copies(gsq.at[side], gs.at[side], gr.at[side]))
        norm = gsq[side, 0]
        for j in range(1, C):
            norm = norm + gsq[side, j]
        alpha = jnp.sqrt(norm + EPS)
        inv = spread(1.0 / alpha, RB)
        back = spread(alpha / beta, RB)
        finish(cell_copies(fq.at[side], fs.at[side], fr.at[side]))
        units = [unit(fq[side, j, B], N, RB) for j in range(C)]
        for b in range(B):
            total = decode(fq[side, 0, b], N) * units[0]
            for j in range(1, C):
                total = total + decode(fq[side, j, b], N) * units[j]
            value = total * inv - back * u[b]
            u[b] = value
            hi, lo = split(value)
            ucat[b, 0:N] = hi
            ucat[b, N:2 * N] = lo
        return alpha

    def step_w(alpha, sine, rho):
        inv = spread(1.0 / alpha, CB)
        ratio = spread(sine * alpha / rho, CB)
        for k in range(NB):
            w[k] = vdec[k] * inv - ratio * w[k]

    def rotate(beta, rhobar, phibar):
        rho = jnp.sqrt(rhobar * rhobar + beta * beta)
        cosine = rhobar / rho
        sine = beta / rho
        phi = cosine * phibar
        return rho, cosine, sine, sine * phibar, phi / rho

    def flip():
        def one(i, carry):
            for s in range(S):
                flipped[i, s] = tiles[i, s].T
            return carry

        lax.fori_loop(0, B, one, 0)

    adjoint(True)
    pl.semaphore_wait(barrier, (C - 1) + (R - 1))
    norm_start()
    start(scatter_copies())
    flip()
    beta = norm_end()
    one = jnp.ones((N, LANES), F32)
    gather(beta, one, lambda: None)

    def body(step, carry):
        beta, cosine, sine, rho, phibar = carry
        alpha = forward(beta, lax.rem(step, 2))
        norm_start()
        adjoint(False)
        start(scatter_copies())
        step_w(alpha, sine, rho)
        beta = norm_end()
        rho, cosine, sine, phibar, length = rotate(beta, -cosine * alpha, phibar)

        def step_x():
            scale = spread(length, CB)
            for k in range(NB):
                x[k] = x[k] + scale * w[k]

        gather(beta, alpha, step_x)
        return beta, cosine, sine, rho, phibar

    carry = (beta, -one, jnp.zeros((N, LANES), F32), one, beta)
    beta, cosine, sine, rho, phibar = lax.fori_loop(0, ITERS - 1, body, carry)
    alpha = forward(beta, (ITERS - 1) % 2)
    norm_start()
    step_w(alpha, sine, rho)
    beta = norm_end()
    rho, cosine, sine, phibar, length = rotate(beta, -cosine * alpha, phibar)
    scale = spread(length, CB)
    for k in range(NB):
        out[:, k * CB:(k + 1) * CB] = x[k] + scale * w[k]
    mis[...] = phibar


def local(R, C, right_side, tiles, pattern, counts):
    N, rows = right_side.shape
    B, S, RB, CB = tiles.shape
    NB = BLK_DEV
    K = NB // R
    slots = B * S
    H = CB // LANES
    assert RB == CB and NB % R == 0
    vmem = pl.BlockSpec(memory_space=pltpu.VMEM)
    hbm = pl.BlockSpec(memory_space=pl.ANY)
    dma = pltpu.SemaphoreType.DMA
    x, mis = pl.pallas_call(
        functools.partial(kernel, R, C),
        out_shape=(
            jax.ShapeDtypeStruct((N, NB * CB), F32),
            jax.ShapeDtypeStruct((N, LANES), F32),
        ),
        in_specs=[hbm, hbm, vmem, hbm],
        out_specs=(vmem, vmem),
        scratch_shapes=[
            pltpu.VMEM((B, S, RB, CB), BF16),
            pltpu.VMEM((B, S, CB, RB), BF16),
            pltpu.VMEM((B, N, RB), F32),
            pltpu.VMEM((2, C, B + 1, N * H, LANES), I16),
            pltpu.VMEM((B, N, RB), F32),
            pltpu.VMEM((B, 2 * N, RB), BF16),
            pltpu.VMEM((R, K + 1, N * H, LANES), I16),
            pltpu.VMEM((R, K + 1, N * H, LANES), I16),
            pltpu.VMEM((R, K + 1, N * H, LANES), I16),
            pltpu.VMEM((NB, N, CB), F32),
            pltpu.VMEM((NB + 1, N, CB), BF16),
            pltpu.VMEM((K, N, CB), F32),
            pltpu.VMEM((R, N, LANES), F32),
            pltpu.VMEM((2, C, N, LANES), F32),
            pltpu.VMEM((slots + 1, N, CB), F32),
            pltpu.VMEM((NB, N, CB), F32),
            pltpu.VMEM((NB, N, CB), F32),
            pltpu.SMEM((S, B), jnp.int32),
            pltpu.SMEM((1, B), jnp.int32),
            pltpu.SMEM((slots,), jnp.int32),
            pltpu.SMEM((slots,), jnp.int32),
            pltpu.SMEM((NB,), jnp.int32),
            dma((B,)), dma((2,)),
            dma((2, C)), dma((2, C)),
            dma((R,)), dma((R,)), dma((R,)), dma((R,)),
            dma((R,)), dma((R,)), dma((2, C)), dma((2, C)),
        ],
        compiler_params=pltpu.CompilerParams(collective_id=0, has_side_effects=True),
    )(pattern.T, counts.T, right_side, tiles)
    return x, mis[:, 0]


def solution(mesh):
    R, C = mesh.shape["ray"], mesh.shape["cell"]
    in_specs = (P(None, "ray"), P("ray", "cell", None, None), P("ray", "cell"), P("ray", "cell"))
    out_specs = (P(None, "cell"), P())
    return jax.shard_map(
        functools.partial(local, R, C), mesh=mesh, in_specs=in_specs, out_specs=out_specs, check_vma=False
    )
```

```python
import functools

import jax
import jax.numpy as jnp
from jax import lax
from jax.experimental import pallas as pl
from jax.experimental.pallas import tpu as pltpu
from jax.sharding import PartitionSpec as P

BLK_DEV = 32
ITERS = 4
EPS = 1e-06
PIECES = 1
CUTS = 1
F32 = jnp.float32
BF16 = jnp.bfloat16
I16 = jnp.int16
LANES = 128
STEPS = 64.0
TOP = 32700.0


def split(value):
    hi = value.astype(BF16)
    lo = (value - hi.astype(F32)).astype(BF16)
    return hi, lo


def spread(stat, lanes):
    return jnp.concatenate([stat] * (lanes // LANES), axis=1)


def total_of(value):
    total = jnp.sum(value, axis=1, keepdims=True)
    return jnp.broadcast_to(total, (value.shape[0], LANES))


def stack(value):
    return jnp.concatenate([value[:, j:j + LANES] for j in range(0, value.shape[1], LANES)], axis=0)


def unstack(value, rows):
    return jnp.concatenate([value[j:j + rows] for j in range(0, value.shape[0], rows)], axis=1)


def range_code(top):
    top = jnp.broadcast_to(jnp.max(top, axis=1, keepdims=True), (top.shape[0], LANES))
    return jnp.ceil(jnp.log2(jnp.maximum(top, 1e-30)) * STEPS) + 1.0


def code_slab(code, lanes):
    return jnp.concatenate([code] * (lanes // LANES), axis=0).astype(jnp.int32).astype(I16)


def encode(value, code):
    share = value * spread(TOP * jnp.exp2(code * (-1.0 / STEPS)), value.shape[1])
    return stack(jnp.round(share)).astype(jnp.int32).astype(I16)


def unit(slab, rows, lanes):
    code = slab[0:rows].astype(jnp.int32).astype(F32)
    return spread(jnp.exp2(code * (1.0 / STEPS)) * (1.0 / TOP), lanes)


def decode(slab, rows):
    return unstack(slab.astype(jnp.int32).astype(F32), rows)


def flipped_bits(me, d):
    peer = me
    bit = 1
    while bit <= d:
        if d // bit % 2:
            peer = peer + bit - 2 * bit * lax.rem(me // bit, 2)
        bit *= 2
    return peer


def partners(me, n):
    if n & (n - 1) == 0:
        return [(d, flipped_bits(me, d)) for d in range(n - 1, 0, -1)]
    return [(d, lax.rem(me + d, n)) for d in range(1, n)]


def kernel(
    R, C,
    pattern_hbm, counts_hbm, rhs, tiles_hbm,
    out, mis,
    tiles, flipped, fpart, fq, u, ucat, aq, arecv, hq, vdec, vb, vsh, usq, gsq, cum, w, x,
    pattern, counts, idx, links_v, links,
    tile_sem, small_sem, fs, fr, as_, ar, ns, nr, hs, hr, gs, gr,
):
    S, B = pattern.shape
    N = rhs.shape[0]
    RB, CB = tiles.shape[2], tiles.shape[3]
    NB = BLK_DEV
    K = NB // R
    P, KP = aq.shape[1], aq.shape[2] - 1
    Q, BQ = fq.shape[2], fq.shape[3] - 1
    slots = B * S
    me_r = lax.axis_index("ray")
    me_c = lax.axis_index("cell")
    ray = partners(me_r, R)
    cell = partners(me_c, C)

    small = [
        pltpu.make_async_copy(pattern_hbm, pattern, small_sem.at[0]),
        pltpu.make_async_copy(counts_hbm, counts, small_sem.at[1]),
    ]
    for copy in small:
        copy.start()
    loads = []
    for b in range(B):
        load = pltpu.make_async_copy(tiles_hbm.at[b], tiles.at[b], tile_sem.at[b])
        load.start()
        loads.append(load)

    barrier = pltpu.get_barrier_semaphore()
    for axis, others in (("cell", cell), ("ray", ray)):
        for _, peer in others:
            pl.semaphore_signal(barrier, inc=1, device_id={axis: peer}, device_id_type=pl.DeviceIdType.MESH)

    def remote(src, dst, send, recv, axis, peer):
        return pltpu.make_async_remote_copy(
            src_ref=src, dst_ref=dst, send_sem=send, recv_sem=recv,
            device_id={axis: peer}, device_id_type=pl.DeviceIdType.MESH,
        )

    cum[slots] = jnp.zeros((N, CB), F32)
    vb[NB] = jnp.zeros((N, CB), BF16)
    w[...] = jnp.zeros_like(w)
    x[...] = jnp.zeros_like(x)
    vsh[...] = jnp.zeros_like(vsh)
    for b in range(B):
        value = rhs[:, b * RB:(b + 1) * RB]
        u[b] = value
        hi, lo = split(value)
        ucat[b, 0:N] = hi
        ucat[b, N:2 * N] = lo

    for copy in small:
        copy.wait()
    for b in range(B):
        for s in range(S):
            idx[b * S + s] = jnp.where(s < counts[0, b], pattern[s, b], NB)

    lane = lax.broadcasted_iota(jnp.int32, (8, LANES), 1)
    sub = lax.broadcasted_iota(jnp.int32, (8, LANES), 0)
    across = jnp.full((8, LANES), -1, jnp.int32)
    for i in range(slots):
        across = jnp.where(lane == i, idx[i], across)
    before = jnp.full((8, LANES), -1, jnp.int32)
    last = jnp.full((8, LANES), -1, jnp.int32)
    for j in range(0, slots, 8):
        down = jnp.full((8, LANES), -1, jnp.int32)
        for i in range(8):
            down = jnp.where(sub == i, idx[j + i], down)
        before = jnp.where((down == across) & (sub + j < lane), sub + j, before)
        last = jnp.where(down == lane, sub + j, last)
    before = jnp.max(before, axis=0, keepdims=True)
    last = jnp.max(last, axis=0, keepdims=True)
    links_v[0:1] = jnp.where(before < 0, slots, before)
    links_v[1:2] = jnp.where(last < 0, slots, last)
    table = pltpu.make_async_copy(links_v, links, small_sem.at[2])
    table.start()
    table.wait()

    def norm_copies():
        return [remote(usq.at[me_r], usq.at[me_r], ns.at[d], nr.at[d], "ray", peer) for d, peer in ray]

    def spread_copies(p):
        own = hq.at[me_r, p]
        return [remote(own, own, hs.at[d, p], hr.at[d, p], "ray", peer) for d, peer in ray]

    def scatter_copies(p):
        return [remote(aq.at[peer, p], arecv.at[d, p], as_.at[d, p], ar.at[d, p], "ray", peer) for d, peer in ray]

    def alpha_copies(side):
        own = gsq.at[side, me_c]
        return [remote(own, own, gs.at[side, d], gr.at[side, d], "cell", peer) for d, peer in cell]

    def time_copies(side, q):
        own = fq.at[side, me_c, q]
        return [remote(own, own, fs.at[side, d, q], fr.at[side, d, q], "cell", peer) for d, peer in cell]

    def start(copies):
        for copy in copies:
            copy.start()

    def finish(copies):
        for copy in copies:
            copy.wait()

    def norm_start():
        sq = jnp.zeros((N, RB), F32)
        for b in range(B):
            sq = sq + u[b] * u[b]
        return total_of(sq)

    def norm_send(total):
        usq[me_r] = total
        start(norm_copies())

    def norm_end():
        finish(norm_copies())
        total = usq[0]
        for r in range(1, R):
            total = total + usq[r]
        return jnp.sqrt(total + EPS)

    def adjoint(wait, norm=None):
        for b in range(B):
            if wait:
                loads[b].wait()
            if norm is not None and b == B // 2:
                norm_send(norm)
            rows = ucat[b]
            for s in range(S):
                i = b * S + s
                per = lax.dot_general(rows, tiles[b, s], (((1,), (0,)), ((), ())), preferred_element_type=F32)
                cum[i] = per[0:N] + per[N:2 * N] + cum[links[0, i]]
        top = jnp.zeros((N, CB), F32)
        for k in range(NB):
            top = jnp.maximum(top, jnp.abs(cum[links[1, k]]))
        code = range_code(top)
        slab = code_slab(code, CB)
        for p in range(P):
            for r in range(R):
                for k in range(KP):
                    aq[r, p, k] = encode(cum[links[1, r * K + p * KP + k]], code)
                aq[r, p, KP] = slab

    def scatter_start():
        for p in range(P):
            start(scatter_copies(p))

    def gather(beta, alpha, beside):
        inv = spread(1.0 / beta, CB)
        back = spread(beta / alpha, CB)
        for p in range(P):
            for copy in scatter_copies(p):
                copy.wait_recv()
            units = {d: unit(arecv[d, p, KP], N, CB) for d, _ in ray}
            top = jnp.zeros((N, CB), F32)
            for k in range(KP):
                total = cum[links[1, me_r * K + p * KP + k]]
                for d, _ in ray:
                    total = total + decode(arecv[d, p, k], N) * units[d]
                v = total * inv - back * vsh[p * KP + k]
                vsh[p * KP + k] = v
                top = jnp.maximum(top, jnp.abs(v))
            code = range_code(top)
            hq[me_r, p, KP] = code_slab(code, CB)
            for k in range(KP):
                hq[me_r, p, k] = encode(vsh[p * KP + k], code)
            start(spread_copies(p))
        for p in range(P):
            for copy in scatter_copies(p):
                copy.wait_send()
        beside()

    def forward(beta, side):
        sq = jnp.zeros((N, CB), F32)
        for p in range(P):
            finish(spread_copies(p))
            for r in range(R):
                grain = unit(hq[r, p, KP], N, CB)
                for k in range(KP):
                    v = decode(hq[r, p, k], N) * grain
                    vdec[r * K + p * KP + k] = v
                    vb[r * K + p * KP + k] = v.astype(BF16)
                    sq = sq + v * v
        sq = total_of(sq)
        for q in range(Q):
            top = jnp.zeros((N, RB), F32)
            for b in range(q * BQ, (q + 1) * BQ):
                if b == B // 2:
                    gsq[side, me_c] = sq
                    start(alpha_copies(side))
                acc = jnp.zeros((N, RB), F32)
                for s in range(S):
                    acc = acc + lax.dot_general(
                        vb[idx[b * S + s]], flipped[b, s], (((1,), (0,)), ((), ())), preferred_element_type=F32
                    )
                fpart[b] = acc
                top = jnp.maximum(top, jnp.abs(acc))
            code = range_code(top)
            fq[side, me_c, q, BQ] = code_slab(code, RB)
            for b in range(BQ):
                fq[side, me_c, q, b] = encode(fpart[q * BQ + b], code)
            start(time_copies(side, q))
        finish(alpha_copies(side))
        norm = gsq[side, 0]
        for j in range(1, C):
            norm = norm + gsq[side, j]
        alpha = jnp.sqrt(norm + EPS)
        inv = spread(1.0 / alpha, RB)
        back = spread(alpha / beta, RB)
        for q in range(Q):
            finish(time_copies(side, q))
            units = [unit(fq[side, j, q, BQ], N, RB) for j in range(C)]
            for b in range(q * BQ, (q + 1) * BQ):
                total = decode(fq[side, 0, q, b - q * BQ], N) * units[0]
                for j in range(1, C):
                    total = total + decode(fq[side, j, q, b - q * BQ], N) * units[j]
                value = total * inv - back * u[b]
                u[b] = value
                hi, lo = split(value)
                ucat[b, 0:N] = hi
                ucat[b, N:2 * N] = lo
        return alpha

    def step_w(alpha, sine, rho):
        inv = spread(1.0 / alpha, CB)
        ratio = spread(sine * alpha / rho, CB)
        for k in range(NB):
            w[k] = vdec[k] * inv - ratio * w[k]

    def rotate(beta, rhobar, phibar):
        rho = jnp.sqrt(rhobar * rhobar + beta * beta)
        cosine = rhobar / rho
        sine = beta / rho
        phi = cosine * phibar
        return rho, cosine, sine, sine * phibar, phi / rho

    def flip():
        def one(i, carry):
            for s in range(S):
                flipped[i, s] = tiles[i, s].T
            return carry

        lax.fori_loop(0, B, one, 0)

    adjoint(True)
    pl.semaphore_wait(barrier, (C - 1) + (R - 1))
    norm_send(norm_start())
    scatter_start()
    flip()
    beta = norm_end()
    one = jnp.ones((N, LANES), F32)
    gather(beta, one, lambda: None)

    def body(step, carry):
        beta, cosine, sine, rho, phibar = carry
        alpha = forward(beta, lax.rem(step, 2))
        adjoint(False, norm_start())
        scatter_start()
        step_w(alpha, sine, rho)
        beta = norm_end()
        rho, cosine, sine, phibar, length = rotate(beta, -cosine * alpha, phibar)

        def step_x():
            scale = spread(length, CB)
            for k in range(NB):
                x[k] = x[k] + scale * w[k]

        gather(beta, alpha, step_x)
        return beta, cosine, sine, rho, phibar

    carry = (beta, -one, jnp.zeros((N, LANES), F32), one, beta)
    beta, cosine, sine, rho, phibar = lax.fori_loop(0, ITERS - 1, body, carry)
    alpha = forward(beta, (ITERS - 1) % 2)
    norm_send(norm_start())
    step_w(alpha, sine, rho)
    beta = norm_end()
    rho, cosine, sine, phibar, length = rotate(beta, -cosine * alpha, phibar)
    scale = spread(length, CB)
    for k in range(NB):
        out[:, k * CB:(k + 1) * CB] = x[k] + scale * w[k]
    mis[...] = phibar


def closing(x_ref, m_ref, out_ref, mis_ref):
    out_ref[...] = x_ref[...]
    for n in range(m_ref.shape[0]):
        mis_ref[n] = m_ref[n, 0]


def local(R, C, right_side, tiles, pattern, counts):
    N, rows = right_side.shape
    B, S, RB, CB = tiles.shape
    NB = BLK_DEV
    K = NB // R
    slots = B * S
    H = CB // LANES
    pieces = PIECES if K % PIECES == 0 else 1
    Q = CUTS if B % CUTS == 0 else 1
    assert RB == CB and NB % R == 0 and NB <= LANES and slots <= LANES and slots % 8 == 0
    vmem = pl.BlockSpec(memory_space=pltpu.VMEM)
    hbm = pl.BlockSpec(memory_space=pl.ANY)
    dma = pltpu.SemaphoreType.DMA
    x, mis = pl.pallas_call(
        functools.partial(kernel, R, C),
        out_shape=(
            jax.ShapeDtypeStruct((N, NB * CB), F32),
            jax.ShapeDtypeStruct((N, LANES), F32),
        ),
        in_specs=[hbm, hbm, vmem, hbm],
        out_specs=(vmem, vmem),
        scratch_shapes=[
            pltpu.VMEM((B, S, RB, CB), BF16),
            pltpu.VMEM((B, S, CB, RB), BF16),
            pltpu.VMEM((B, N, RB), F32),
            pltpu.VMEM((2, C, Q, B // Q + 1, N * H, LANES), I16),
            pltpu.VMEM((B, N, RB), F32),
            pltpu.VMEM((B, 2 * N, RB), BF16),
            pltpu.VMEM((R, pieces, K // pieces + 1, N * H, LANES), I16),
            pltpu.VMEM((R, pieces, K // pieces + 1, N * H, LANES), I16),
            pltpu.VMEM((R, pieces, K // pieces + 1, N * H, LANES), I16),
            pltpu.VMEM((NB, N, CB), F32),
            pltpu.VMEM((NB + 1, N, CB), BF16),
            pltpu.VMEM((K, N, CB), F32),
            pltpu.VMEM((R, N, LANES), F32),
            pltpu.VMEM((2, C, N, LANES), F32),
            pltpu.VMEM((slots + 1, N, CB), F32),
            pltpu.VMEM((NB, N, CB), F32),
            pltpu.VMEM((NB, N, CB), F32),
            pltpu.SMEM((S, B), jnp.int32),
            pltpu.SMEM((1, B), jnp.int32),
            pltpu.SMEM((slots,), jnp.int32),
            pltpu.VMEM((2, LANES), jnp.int32),
            pltpu.SMEM((2, LANES), jnp.int32),
            dma((B,)), dma((3,)),
            dma((2, C, Q)), dma((2, C, Q)),
            dma((R, pieces)), dma((R, pieces)), dma((R,)), dma((R,)),
            dma((R, pieces)), dma((R, pieces)), dma((2, C)), dma((2, C)),
        ],
        compiler_params=pltpu.CompilerParams(collective_id=0, has_side_effects=True),
    )(pattern.T, counts.T, right_side, tiles)
    smem = pl.BlockSpec(memory_space=pltpu.SMEM)
    return pl.pallas_call(
        closing,
        out_shape=(jax.ShapeDtypeStruct(x.shape, F32), jax.ShapeDtypeStruct((N,), F32)),
        in_specs=[vmem, smem],
        out_specs=(vmem, smem),
    )(x, mis)


def solution(mesh):
    R, C = mesh.shape["ray"], mesh.shape["cell"]
    in_specs = (P(None, "ray"), P("ray", "cell", None, None), P("ray", "cell"), P("ray", "cell"))
    out_specs = (P(None, "cell"), P())
    return jax.shard_map(
        functools.partial(local, R, C), mesh=mesh, in_specs=in_specs, out_specs=out_specs, check_vma=False
    )
```

```python
import functools

import jax
import jax.numpy as jnp
from jax import lax
from jax.experimental import pallas as pl
from jax.experimental.pallas import tpu as pltpu
from jax.sharding import PartitionSpec as P

BLK_DEV = 32
ITERS = 4
EPS = 1e-06
PIECES = 1
CUTS = 1
F32 = jnp.float32
BF16 = jnp.bfloat16
I16 = jnp.int16
LANES = 128
STEPS = 64.0
TOP = 32700.0


def split(value):
    hi = value.astype(BF16)
    lo = (value - hi.astype(F32)).astype(BF16)
    return hi, lo


def spread(stat, lanes):
    return jnp.concatenate([stat] * (lanes // LANES), axis=1)


def total_of(value):
    total = jnp.sum(value, axis=1, keepdims=True)
    return jnp.broadcast_to(total, (value.shape[0], LANES))


def diagonal(value, rows, axis):
    here = lax.broadcasted_iota(jnp.int32, (rows, LANES), 0) == lax.broadcasted_iota(jnp.int32, (rows, LANES), 1)
    return jnp.sum(jnp.where(here, value, 0.0), axis=axis, keepdims=True)


def to_row(stat):
    return diagonal(stat, stat.shape[0], 0)


def from_row(row, rows):
    return jnp.broadcast_to(diagonal(jnp.broadcast_to(row, (rows, LANES)), rows, 1), (rows, LANES))


def range_code(top):
    top = jnp.broadcast_to(jnp.max(top, axis=1, keepdims=True), (top.shape[0], LANES))
    return jnp.ceil(jnp.log2(jnp.maximum(top, 1e-30)) * STEPS) + 1.0


def put_code(message, code):
    message[message.shape[0] - 1] = code.astype(jnp.int32).astype(I16)


def put(message, k, value, code):
    parts = value.shape[1] // LANES
    scale = TOP * jnp.exp2(code * (-1.0 / STEPS))
    for j in range(parts):
        share = jnp.round(value[:, j * LANES:(j + 1) * LANES] * scale)
        message[k * parts + j] = share.astype(jnp.int32).astype(I16)


def unit(message, lanes):
    code = message[message.shape[0] - 1].astype(jnp.int32).astype(F32)
    return spread(jnp.exp2(code * (1.0 / STEPS)) * (1.0 / TOP), lanes)


def take(message, k, lanes):
    parts = lanes // LANES
    return jnp.concatenate([message[k * parts + j].astype(jnp.int32).astype(F32) for j in range(parts)], axis=1)


def flipped_bits(me, d):
    peer = me
    bit = 1
    while bit <= d:
        if d // bit % 2:
            peer = peer + bit - 2 * bit * lax.rem(me // bit, 2)
        bit *= 2
    return peer


def partners(me, n):
    if n & (n - 1) == 0:
        return [(d, flipped_bits(me, d)) for d in range(n - 1, 0, -1)]
    return [(d, lax.rem(me + d, n)) for d in range(1, n)]


def kernel(
    R, C,
    pattern_hbm, counts_hbm, rhs_hbm, tiles_hbm,
    out, mis,
    rhs, tiles, flipped, fpart, fq, u, ucat, aq, arecv, hq, vdec, vb, vsh, usq, gsq, cum, w, x,
    pattern, counts, idx, links_v, links,
    tile_sem, small_sem, fs, fr, as_, ar, ns, nr, hs, hr, gs, gr,
):
    S, B = pattern.shape
    N = rhs.shape[0]
    RB, CB = tiles.shape[2], tiles.shape[3]
    NB = BLK_DEV
    K = NB // R
    P, Q = aq.shape[1], fq.shape[2]
    KP, BQ = K // P, B // Q
    slots = B * S
    me_r = lax.axis_index("ray")
    me_c = lax.axis_index("cell")
    ray = partners(me_r, R)
    cell = partners(me_c, C)

    small = [
        pltpu.make_async_copy(pattern_hbm, pattern, small_sem.at[0]),
        pltpu.make_async_copy(counts_hbm, counts, small_sem.at[1]),
    ]
    seen = pltpu.make_async_copy(rhs_hbm, rhs, small_sem.at[3])
    for copy in small:
        copy.start()
    seen.start()
    loads = []
    for b in range(B):
        load = pltpu.make_async_copy(tiles_hbm.at[b], tiles.at[b], tile_sem.at[b])
        load.start()
        loads.append(load)

    barrier = pltpu.get_barrier_semaphore()
    for axis, others in (("cell", cell), ("ray", ray)):
        for _, peer in others:
            pl.semaphore_signal(barrier, inc=1, device_id={axis: peer}, device_id_type=pl.DeviceIdType.MESH)

    def remote(src, dst, send, recv, axis, peer):
        return pltpu.make_async_remote_copy(
            src_ref=src, dst_ref=dst, send_sem=send, recv_sem=recv,
            device_id={axis: peer}, device_id_type=pl.DeviceIdType.MESH,
        )

    cum[slots] = jnp.zeros((N, CB), F32)
    vb[NB] = jnp.zeros((N, CB), BF16)
    w[...] = jnp.zeros_like(w)
    x[...] = jnp.zeros_like(x)
    vsh[...] = jnp.zeros_like(vsh)
    for copy in small:
        copy.wait()
    for b in range(B):
        for s in range(S):
            idx[b * S + s] = jnp.where(s < counts[0, b], pattern[s, b], NB)

    lane = lax.broadcasted_iota(jnp.int32, (8, LANES), 1)
    sub = lax.broadcasted_iota(jnp.int32, (8, LANES), 0)
    across = jnp.full((8, LANES), -1, jnp.int32)
    for i in range(slots):
        across = jnp.where(lane == i, idx[i], across)
    before = jnp.full((8, LANES), -1, jnp.int32)
    last = jnp.full((8, LANES), -1, jnp.int32)
    for j in range(0, slots, 8):
        down = jnp.full((8, LANES), -1, jnp.int32)
        for i in range(8):
            down = jnp.where(sub == i, idx[j + i], down)
        before = jnp.where((down == across) & (sub + j < lane), sub + j, before)
        last = jnp.where(down == lane, sub + j, last)
    before = jnp.max(before, axis=0, keepdims=True)
    last = jnp.max(last, axis=0, keepdims=True)
    links_v[0:1] = jnp.where(before < 0, slots, before)
    links_v[1:2] = jnp.where(last < 0, slots, last)
    table = pltpu.make_async_copy(links_v, links, small_sem.at[2])
    table.start()
    seen.wait()
    for b in range(B):
        value = rhs[:, b * RB:(b + 1) * RB]
        u[b] = value
        hi, lo = split(value)
        ucat[b, 0:N] = hi
        ucat[b, N:2 * N] = lo
    table.wait()

    def norm_copies():
        return [remote(usq.at[me_r], usq.at[me_r], ns.at[d], nr.at[d], "ray", peer) for d, peer in ray]

    def spread_copies(p):
        own = hq.at[me_r, p]
        return [remote(own, own, hs.at[d, p], hr.at[d, p], "ray", peer) for d, peer in ray]

    def scatter_copies(p):
        return [remote(aq.at[peer, p], arecv.at[d, p], as_.at[d, p], ar.at[d, p], "ray", peer) for d, peer in ray]

    def alpha_copies(side):
        own = gsq.at[side, me_c]
        return [remote(own, own, gs.at[side, d], gr.at[side, d], "cell", peer) for d, peer in cell]

    def time_copies(side, q):
        own = fq.at[side, me_c, q]
        return [remote(own, own, fs.at[side, d, q], fr.at[side, d, q], "cell", peer) for d, peer in cell]

    def start(copies):
        for copy in copies:
            copy.start()

    def finish(copies):
        for copy in copies:
            copy.wait()

    def norm_start():
        sq = jnp.zeros((N, RB), F32)
        for b in range(B):
            sq = sq + u[b] * u[b]
        return to_row(total_of(sq))

    def norm_send(total):
        usq[me_r] = total
        start(norm_copies())

    def norm_end():
        finish(norm_copies())
        total = usq[0]
        for r in range(1, R):
            total = total + usq[r]
        return jnp.sqrt(from_row(total, N) + EPS)

    def adjoint(wait, norm=None):
        for b in range(B):
            if wait:
                loads[b].wait()
            if norm is not None and b == B // 2:
                norm_send(norm)
            rows = ucat[b]
            for s in range(S):
                i = b * S + s
                per = lax.dot_general(rows, tiles[b, s], (((1,), (0,)), ((), ())), preferred_element_type=F32)
                cum[i] = per[0:N] + per[N:2 * N] + cum[links[0, i]]
        top = jnp.zeros((N, CB), F32)
        for k in range(NB):
            top = jnp.maximum(top, jnp.abs(cum[links[1, k]]))
        code = range_code(top)
        for p in range(P):
            for r in range(R):
                for k in range(KP):
                    put(aq.at[r, p], k, cum[links[1, r * K + p * KP + k]], code)
                put_code(aq.at[r, p], code)

    def scatter_start():
        for p in range(P):
            start(scatter_copies(p))

    def gather(beta, alpha, beside):
        inv = spread(1.0 / beta, CB)
        back = spread(beta / alpha, CB)
        for p in range(P):
            for copy in scatter_copies(p):
                copy.wait_recv()
            units = {d: unit(arecv.at[d, p], CB) for d, _ in ray}
            top = jnp.zeros((N, CB), F32)
            for k in range(KP):
                total = cum[links[1, me_r * K + p * KP + k]]
                for d, _ in ray:
                    total = total + take(arecv.at[d, p], k, CB) * units[d]
                v = total * inv - back * vsh[p * KP + k]
                vsh[p * KP + k] = v
                top = jnp.maximum(top, jnp.abs(v))
            code = range_code(top)
            put_code(hq.at[me_r, p], code)
            for k in range(KP):
                put(hq.at[me_r, p], k, vsh[p * KP + k], code)
            start(spread_copies(p))
        for p in range(P):
            for copy in scatter_copies(p):
                copy.wait_send()
        beside()

    def forward(beta, side):
        sq = jnp.zeros((N, CB), F32)
        for p in range(P):
            finish(spread_copies(p))
            for r in range(R):
                grain = unit(hq.at[r, p], CB)
                for k in range(KP):
                    v = take(hq.at[r, p], k, CB) * grain
                    vdec[r * K + p * KP + k] = v
                    vb[r * K + p * KP + k] = v.astype(BF16)
                    sq = sq + v * v
        sq = to_row(total_of(sq))
        for q in range(Q):
            top = jnp.zeros((N, RB), F32)
            for b in range(q * BQ, (q + 1) * BQ):
                if b == B // 2:
                    gsq[side, me_c] = sq
                    start(alpha_copies(side))
                acc = jnp.zeros((N, RB), F32)
                for s in range(S):
                    acc = acc + lax.dot_general(
                        vb[idx[b * S + s]], flipped[b, s], (((1,), (0,)), ((), ())), preferred_element_type=F32
                    )
                fpart[b] = acc
                top = jnp.maximum(top, jnp.abs(acc))
            code = range_code(top)
            put_code(fq.at[side, me_c, q], code)
            for b in range(BQ):
                put(fq.at[side, me_c, q], b, fpart[q * BQ + b], code)
            start(time_copies(side, q))
        finish(alpha_copies(side))
        norm = gsq[side, 0]
        for j in range(1, C):
            norm = norm + gsq[side, j]
        alpha = jnp.sqrt(from_row(norm, N) + EPS)
        inv = spread(1.0 / alpha, RB)
        back = spread(alpha / beta, RB)
        for q in range(Q):
            finish(time_copies(side, q))
            units = [unit(fq.at[side, j, q], RB) for j in range(C)]
            for b in range(q * BQ, (q + 1) * BQ):
                total = take(fq.at[side, 0, q], b - q * BQ, RB) * units[0]
                for j in range(1, C):
                    total = total + take(fq.at[side, j, q], b - q * BQ, RB) * units[j]
                value = total * inv - back * u[b]
                u[b] = value
                hi, lo = split(value)
                ucat[b, 0:N] = hi
                ucat[b, N:2 * N] = lo
        return alpha

    def step_w(alpha, sine, rho):
        inv = spread(1.0 / alpha, CB)
        ratio = spread(sine * alpha / rho, CB)
        for k in range(NB):
            w[k] = vdec[k] * inv - ratio * w[k]

    def rotate(beta, rhobar, phibar):
        rho = jnp.sqrt(rhobar * rhobar + beta * beta)
        cosine = rhobar / rho
        sine = beta / rho
        phi = cosine * phibar
        return rho, cosine, sine, sine * phibar, phi / rho

    def flip():
        def one(i, carry):
            for s in range(S):
                flipped[i, s] = tiles[i, s].T
            return carry

        lax.fori_loop(0, B, one, 0)

    adjoint(True)
    pl.semaphore_wait(barrier, (C - 1) + (R - 1))
    norm_send(norm_start())
    scatter_start()
    flip()
    beta = norm_end()
    one = jnp.ones((N, LANES), F32)
    gather(beta, one, lambda: None)

    def body(step, carry):
        beta, cosine, sine, rho, phibar = carry
        alpha = forward(beta, lax.rem(step, 2))
        adjoint(False, norm_start())
        scatter_start()
        step_w(alpha, sine, rho)
        beta = norm_end()
        rho, cosine, sine, phibar, length = rotate(beta, -cosine * alpha, phibar)

        def step_x():
            scale = spread(length, CB)
            for k in range(NB):
                x[k] = x[k] + scale * w[k]

        gather(beta, alpha, step_x)
        return beta, cosine, sine, rho, phibar

    carry = (beta, -one, jnp.zeros((N, LANES), F32), one, beta)
    beta, cosine, sine, rho, phibar = lax.fori_loop(0, ITERS - 1, body, carry)
    alpha = forward(beta, (ITERS - 1) % 2)
    norm_send(norm_start())
    step_w(alpha, sine, rho)
    beta = norm_end()
    rho, cosine, sine, phibar, length = rotate(beta, -cosine * alpha, phibar)
    scale = spread(length, CB)
    for k in range(NB):
        out[:, k * CB:(k + 1) * CB] = x[k] + scale * w[k]
    mis[...] = phibar


def closing(x_ref, m_ref, out_ref, mis_ref):
    out_ref[...] = x_ref[...]
    for n in range(m_ref.shape[0]):
        mis_ref[n] = m_ref[n, 0]


def local(R, C, right_side, tiles, pattern, counts):
    N, rows = right_side.shape
    B, S, RB, CB = tiles.shape
    NB = BLK_DEV
    K = NB // R
    slots = B * S
    H = CB // LANES
    pieces = PIECES if K % PIECES == 0 else 1
    Q = CUTS if B % CUTS == 0 else 1
    assert RB == CB and NB % R == 0 and NB <= LANES and slots <= LANES and slots % 8 == 0
    vmem = pl.BlockSpec(memory_space=pltpu.VMEM)
    hbm = pl.BlockSpec(memory_space=pl.ANY)
    dma = pltpu.SemaphoreType.DMA
    x, mis = pl.pallas_call(
        functools.partial(kernel, R, C),
        out_shape=(
            jax.ShapeDtypeStruct((N, NB * CB), F32),
            jax.ShapeDtypeStruct((N, LANES), F32),
        ),
        in_specs=[hbm, hbm, hbm, hbm],
        out_specs=(vmem, vmem),
        scratch_shapes=[
            pltpu.VMEM((N, rows), F32),
            pltpu.VMEM((B, S, RB, CB), BF16),
            pltpu.VMEM((B, S, CB, RB), BF16),
            pltpu.VMEM((B, N, RB), F32),
            pltpu.VMEM((2, C, Q, B // Q * H + 1, N, LANES), I16),
            pltpu.VMEM((B, N, RB), F32),
            pltpu.VMEM((B, 2 * N, RB), BF16),
            pltpu.VMEM((R, pieces, K // pieces * H + 1, N, LANES), I16),
            pltpu.VMEM((R, pieces, K // pieces * H + 1, N, LANES), I16),
            pltpu.VMEM((R, pieces, K // pieces * H + 1, N, LANES), I16),
            pltpu.VMEM((NB, N, CB), F32),
            pltpu.VMEM((NB + 1, N, CB), BF16),
            pltpu.VMEM((K, N, CB), F32),
            pltpu.VMEM((R, 1, LANES), F32),
            pltpu.VMEM((2, C, 1, LANES), F32),
            pltpu.VMEM((slots + 1, N, CB), F32),
            pltpu.VMEM((NB, N, CB), F32),
            pltpu.VMEM((NB, N, CB), F32),
            pltpu.SMEM((S, B), jnp.int32),
            pltpu.SMEM((1, B), jnp.int32),
            pltpu.SMEM((slots,), jnp.int32),
            pltpu.VMEM((2, LANES), jnp.int32),
            pltpu.SMEM((2, LANES), jnp.int32),
            dma((B,)), dma((4,)),
            dma((2, C, Q)), dma((2, C, Q)),
            dma((R, pieces)), dma((R, pieces)), dma((R,)), dma((R,)),
            dma((R, pieces)), dma((R, pieces)), dma((2, C)), dma((2, C)),
        ],
        compiler_params=pltpu.CompilerParams(collective_id=0, has_side_effects=True),
    )(pattern.T, counts.T, right_side, tiles)
    smem = pl.BlockSpec(memory_space=pltpu.SMEM)
    return pl.pallas_call(
        closing,
        out_shape=(jax.ShapeDtypeStruct(x.shape, F32), jax.ShapeDtypeStruct((N,), F32)),
        in_specs=[vmem, smem],
        out_specs=(vmem, smem),
    )(x, mis)


def solution(mesh):
    R, C = mesh.shape["ray"], mesh.shape["cell"]
    in_specs = (P(None, "ray"), P("ray", "cell", None, None), P("ray", "cell"), P("ray", "cell"))
    out_specs = (P(None, "cell"), P())
    return jax.shard_map(
        functools.partial(local, R, C), mesh=mesh, in_specs=in_specs, out_specs=out_specs, check_vma=False
    )
```

```python
import functools

import jax
import jax.numpy as jnp
from jax import lax
from jax.experimental import pallas as pl
from jax.experimental.pallas import tpu as pltpu
from jax.sharding import PartitionSpec as P

BLK_DEV = 32
ITERS = 4
EPS = 1e-06
PIECES = 1
CUTS = 1
F32 = jnp.float32
BF16 = jnp.bfloat16
I16 = jnp.int16
LANES = 128
STEPS = 64.0
TOP = 32700.0


def split(value):
    hi = value.astype(BF16)
    lo = (value - hi.astype(F32)).astype(BF16)
    return hi, lo


def spread(stat, lanes):
    return jnp.concatenate([stat] * (lanes // LANES), axis=1)


def total_of(value):
    total = jnp.sum(value, axis=1, keepdims=True)
    return jnp.broadcast_to(total, (value.shape[0], LANES))


def diagonal(value, rows, axis):
    here = lax.broadcasted_iota(jnp.int32, (rows, LANES), 0) == lax.broadcasted_iota(jnp.int32, (rows, LANES), 1)
    return jnp.sum(jnp.where(here, value, 0.0), axis=axis, keepdims=True)


def to_row(stat):
    return diagonal(stat, stat.shape[0], 0)


def from_row(row, rows):
    return jnp.broadcast_to(diagonal(jnp.broadcast_to(row, (rows, LANES)), rows, 1), (rows, LANES))


def range_code(top):
    top = jnp.broadcast_to(jnp.max(top, axis=1, keepdims=True), (top.shape[0], LANES))
    return jnp.ceil(jnp.log2(jnp.maximum(top, 1e-30)) * STEPS) + 1.0


def put_code(message, code):
    message[message.shape[0] - 1] = code.astype(jnp.int32).astype(I16)


def put(message, k, value, code):
    parts = value.shape[1] // LANES
    scale = TOP * jnp.exp2(code * (-1.0 / STEPS))
    for j in range(parts):
        share = jnp.round(value[:, j * LANES:(j + 1) * LANES] * scale)
        message[k * parts + j] = share.astype(jnp.int32).astype(I16)


def unit(message, lanes):
    code = message[message.shape[0] - 1].astype(jnp.int32).astype(F32)
    return spread(jnp.exp2(code * (1.0 / STEPS)) * (1.0 / TOP), lanes)


def take(message, k, lanes):
    parts = lanes // LANES
    return jnp.concatenate([message[k * parts + j].astype(jnp.int32).astype(F32) for j in range(parts)], axis=1)


def flipped_bits(me, d):
    peer = me
    bit = 1
    while bit <= d:
        if d // bit % 2:
            peer = peer + bit - 2 * bit * lax.rem(me // bit, 2)
        bit *= 2
    return peer


def partners(me, n):
    if n & (n - 1) == 0:
        return [(d, flipped_bits(me, d)) for d in range(n - 1, 0, -1)]
    return [(d, lax.rem(me + d, n)) for d in range(1, n)]


def kernel(
    R, C,
    pattern_hbm, counts_hbm, rhs_hbm, tiles_hbm,
    out, mis,
    rhs, tiles, flipped, fpart, fq, u, ucat, aq, arecv, hq, vdec, vb, vsh, usq, gsq, cum, w, x,
    pattern, counts, idx, links_v, links,
    tile_sem, small_sem, fs, fr, as_, ar, ns, nr, hs, hr, gs, gr,
):
    S, B = pattern.shape
    N = rhs.shape[0]
    RB, CB = tiles.shape[2], tiles.shape[3]
    NB = BLK_DEV
    K = NB // R
    P, Q = aq.shape[1], fq.shape[2]
    KP, BQ = K // P, B // Q
    slots = B * S
    me_r = lax.axis_index("ray")
    me_c = lax.axis_index("cell")
    ray = partners(me_r, R)
    cell = partners(me_c, C)

    small = [
        pltpu.make_async_copy(pattern_hbm, pattern, small_sem.at[0]),
        pltpu.make_async_copy(counts_hbm, counts, small_sem.at[1]),
    ]
    seen = pltpu.make_async_copy(rhs_hbm, rhs, small_sem.at[3])
    for copy in small:
        copy.start()
    seen.start()
    loads = []
    for b in range(B):
        load = pltpu.make_async_copy(tiles_hbm.at[b], tiles.at[b], tile_sem.at[b])
        load.start()
        loads.append(load)

    barrier = pltpu.get_barrier_semaphore()
    for axis, others in (("cell", cell), ("ray", ray)):
        for _, peer in others:
            pl.semaphore_signal(barrier, inc=1, device_id={axis: peer}, device_id_type=pl.DeviceIdType.MESH)

    def remote(src, dst, send, recv, axis, peer):
        return pltpu.make_async_remote_copy(
            src_ref=src, dst_ref=dst, send_sem=send, recv_sem=recv,
            device_id={axis: peer}, device_id_type=pl.DeviceIdType.MESH,
        )

    cum[slots] = jnp.zeros((N, CB), F32)
    vb[NB] = jnp.zeros((2 * N, CB), BF16)
    w[...] = jnp.zeros_like(w)
    x[...] = jnp.zeros_like(x)
    vsh[...] = jnp.zeros_like(vsh)
    for copy in small:
        copy.wait()
    for b in range(B):
        for s in range(S):
            idx[b * S + s] = jnp.where(s < counts[0, b], pattern[s, b], NB)

    lane = lax.broadcasted_iota(jnp.int32, (8, LANES), 1)
    sub = lax.broadcasted_iota(jnp.int32, (8, LANES), 0)
    across = jnp.full((8, LANES), -1, jnp.int32)
    for i in range(slots):
        across = jnp.where(lane == i, idx[i], across)
    before = jnp.full((8, LANES), -1, jnp.int32)
    last = jnp.full((8, LANES), -1, jnp.int32)
    for j in range(0, slots, 8):
        down = jnp.full((8, LANES), -1, jnp.int32)
        for i in range(8):
            down = jnp.where(sub == i, idx[j + i], down)
        before = jnp.where((down == across) & (sub + j < lane), sub + j, before)
        last = jnp.where(down == lane, sub + j, last)
    before = jnp.max(before, axis=0, keepdims=True)
    last = jnp.max(last, axis=0, keepdims=True)
    links_v[0:1] = jnp.where(before < 0, slots, before)
    links_v[1:2] = jnp.where(last < 0, slots, last)
    table = pltpu.make_async_copy(links_v, links, small_sem.at[2])
    table.start()
    seen.wait()
    for b in range(B):
        value = rhs[:, b * RB:(b + 1) * RB]
        u[b] = value
        hi, lo = split(value)
        ucat[b, 0:N] = hi
        ucat[b, N:2 * N] = lo
    table.wait()

    def norm_copies():
        return [remote(usq.at[me_r], usq.at[me_r], ns.at[d], nr.at[d], "ray", peer) for d, peer in ray]

    def spread_copies(p):
        own = hq.at[me_r, p]
        return [remote(own, own, hs.at[d, p], hr.at[d, p], "ray", peer) for d, peer in ray]

    def scatter_copies(p):
        return [remote(aq.at[peer, p], arecv.at[d, p], as_.at[d, p], ar.at[d, p], "ray", peer) for d, peer in ray]

    def alpha_copies(side):
        own = gsq.at[side, me_c]
        return [remote(own, own, gs.at[side, d], gr.at[side, d], "cell", peer) for d, peer in cell]

    def time_copies(side, q):
        own = fq.at[side, me_c, q]
        return [remote(own, own, fs.at[side, d, q], fr.at[side, d, q], "cell", peer) for d, peer in cell]

    def start(copies):
        for copy in copies:
            copy.start()

    def finish(copies):
        for copy in copies:
            copy.wait()

    def norm_start():
        sq = jnp.zeros((N, RB), F32)
        for b in range(B):
            sq = sq + u[b] * u[b]
        return to_row(total_of(sq))

    def norm_send(total):
        usq[me_r] = total
        start(norm_copies())

    def norm_end():
        finish(norm_copies())
        total = usq[0]
        for r in range(1, R):
            total = total + usq[r]
        return jnp.sqrt(from_row(total, N) + EPS)

    def adjoint(wait, norm=None):
        for b in range(B):
            if wait:
                loads[b].wait()
            if norm is not None and b == B // 2:
                norm_send(norm)
            rows = ucat[b]
            for s in range(S):
                i = b * S + s
                per = lax.dot_general(rows, tiles[b, s], (((1,), (0,)), ((), ())), preferred_element_type=F32)
                cum[i] = per[0:N] + per[N:2 * N] + cum[links[0, i]]
        top = jnp.zeros((N, CB), F32)
        for k in range(NB):
            top = jnp.maximum(top, jnp.abs(cum[links[1, k]]))
        code = range_code(top)
        for p in range(P):
            for r in range(R):
                for k in range(KP):
                    put(aq.at[r, p], k, cum[links[1, r * K + p * KP + k]], code)
                put_code(aq.at[r, p], code)

    def scatter_start():
        for p in range(P):
            start(scatter_copies(p))

    def gather(beta, alpha, beside):
        inv = spread(1.0 / beta, CB)
        back = spread(beta / alpha, CB)
        for p in range(P):
            for copy in scatter_copies(p):
                copy.wait_recv()
            units = {d: unit(arecv.at[d, p], CB) for d, _ in ray}
            top = jnp.zeros((N, CB), F32)
            for k in range(KP):
                total = cum[links[1, me_r * K + p * KP + k]]
                for d, _ in ray:
                    total = total + take(arecv.at[d, p], k, CB) * units[d]
                v = total * inv - back * vsh[p * KP + k]
                vsh[p * KP + k] = v
                top = jnp.maximum(top, jnp.abs(v))
            code = range_code(top)
            put_code(hq.at[me_r, p], code)
            for k in range(KP):
                put(hq.at[me_r, p], k, vsh[p * KP + k], code)
            start(spread_copies(p))
        for p in range(P):
            for copy in scatter_copies(p):
                copy.wait_send()
        beside()

    def forward(beta, side):
        sq = jnp.zeros((N, CB), F32)
        for p in range(P):
            finish(spread_copies(p))
            for r in range(R):
                grain = unit(hq.at[r, p], CB)
                for k in range(KP):
                    v = take(hq.at[r, p], k, CB) * grain
                    vdec[r * K + p * KP + k] = v
                    hi, lo = split(v)
                    vb[r * K + p * KP + k, 0:N] = hi
                    vb[r * K + p * KP + k, N:2 * N] = lo
                    sq = sq + v * v
        sq = to_row(total_of(sq))
        for q in range(Q):
            top = jnp.zeros((N, RB), F32)
            for b in range(q * BQ, (q + 1) * BQ):
                if b == B // 2:
                    gsq[side, me_c] = sq
                    start(alpha_copies(side))
                acc = jnp.zeros((2 * N, RB), F32)
                for s in range(S):
                    acc = acc + lax.dot_general(
                        vb[idx[b * S + s]], flipped[b, s], (((1,), (0,)), ((), ())), preferred_element_type=F32
                    )
                acc = acc[0:N] + acc[N:2 * N]
                fpart[b] = acc
                top = jnp.maximum(top, jnp.abs(acc))
            code = range_code(top)
            put_code(fq.at[side, me_c, q], code)
            for b in range(BQ):
                put(fq.at[side, me_c, q], b, fpart[q * BQ + b], code)
            start(time_copies(side, q))
        finish(alpha_copies(side))
        norm = gsq[side, 0]
        for j in range(1, C):
            norm = norm + gsq[side, j]
        alpha = jnp.sqrt(from_row(norm, N) + EPS)
        inv = spread(1.0 / alpha, RB)
        back = spread(alpha / beta, RB)
        for q in range(Q):
            finish(time_copies(side, q))
            units = [unit(fq.at[side, j, q], RB) for j in range(C)]
            for b in range(q * BQ, (q + 1) * BQ):
                total = take(fq.at[side, 0, q], b - q * BQ, RB) * units[0]
                for j in range(1, C):
                    total = total + take(fq.at[side, j, q], b - q * BQ, RB) * units[j]
                value = total * inv - back * u[b]
                u[b] = value
                hi, lo = split(value)
                ucat[b, 0:N] = hi
                ucat[b, N:2 * N] = lo
        return alpha

    def step_w(alpha, sine, rho):
        inv = spread(1.0 / alpha, CB)
        ratio = spread(sine * alpha / rho, CB)
        for k in range(NB):
            w[k] = vdec[k] * inv - ratio * w[k]

    def rotate(beta, rhobar, phibar):
        rho = jnp.sqrt(rhobar * rhobar + beta * beta)
        cosine = rhobar / rho
        sine = beta / rho
        phi = cosine * phibar
        return rho, cosine, sine, sine * phibar, phi / rho

    def flip():
        def one(i, carry):
            for s in range(S):
                flipped[i, s] = tiles[i, s].T
            return carry

        lax.fori_loop(0, B, one, 0)

    adjoint(True)
    pl.semaphore_wait(barrier, (C - 1) + (R - 1))
    norm_send(norm_start())
    scatter_start()
    flip()
    beta = norm_end()
    one = jnp.ones((N, LANES), F32)
    gather(beta, one, lambda: None)

    def body(step, carry):
        beta, cosine, sine, rho, phibar = carry
        alpha = forward(beta, lax.rem(step, 2))
        adjoint(False, norm_start())
        scatter_start()
        step_w(alpha, sine, rho)
        beta = norm_end()
        rho, cosine, sine, phibar, length = rotate(beta, -cosine * alpha, phibar)

        def step_x():
            scale = spread(length, CB)
            for k in range(NB):
                x[k] = x[k] + scale * w[k]

        gather(beta, alpha, step_x)
        return beta, cosine, sine, rho, phibar

    carry = (beta, -one, jnp.zeros((N, LANES), F32), one, beta)
    beta, cosine, sine, rho, phibar = lax.fori_loop(0, ITERS - 1, body, carry)
    alpha = forward(beta, (ITERS - 1) % 2)
    norm_send(norm_start())
    step_w(alpha, sine, rho)
    beta = norm_end()
    rho, cosine, sine, phibar, length = rotate(beta, -cosine * alpha, phibar)
    scale = spread(length, CB)
    for k in range(NB):
        out[:, k * CB:(k + 1) * CB] = x[k] + scale * w[k]
    mis[...] = phibar


def closing(x_ref, m_ref, out_ref, mis_ref):
    out_ref[...] = x_ref[...]
    for n in range(m_ref.shape[0]):
        mis_ref[n] = m_ref[n, 0]


def local(R, C, right_side, tiles, pattern, counts):
    N, rows = right_side.shape
    B, S, RB, CB = tiles.shape
    NB = BLK_DEV
    K = NB // R
    slots = B * S
    H = CB // LANES
    pieces = PIECES if K % PIECES == 0 else 1
    Q = CUTS if B % CUTS == 0 else 1
    assert RB == CB and NB % R == 0 and NB <= LANES and slots <= LANES and slots % 8 == 0
    vmem = pl.BlockSpec(memory_space=pltpu.VMEM)
    hbm = pl.BlockSpec(memory_space=pl.ANY)
    dma = pltpu.SemaphoreType.DMA
    x, mis = pl.pallas_call(
        functools.partial(kernel, R, C),
        out_shape=(
            jax.ShapeDtypeStruct((N, NB * CB), F32),
            jax.ShapeDtypeStruct((N, LANES), F32),
        ),
        in_specs=[hbm, hbm, hbm, hbm],
        out_specs=(vmem, vmem),
        scratch_shapes=[
            pltpu.VMEM((N, rows), F32),
            pltpu.VMEM((B, S, RB, CB), BF16),
            pltpu.VMEM((B, S, CB, RB), BF16),
            pltpu.VMEM((B, N, RB), F32),
            pltpu.VMEM((2, C, Q, B // Q * H + 1, N, LANES), I16),
            pltpu.VMEM((B, N, RB), F32),
            pltpu.VMEM((B, 2 * N, RB), BF16),
            pltpu.VMEM((R, pieces, K // pieces * H + 1, N, LANES), I16),
            pltpu.VMEM((R, pieces, K // pieces * H + 1, N, LANES), I16),
            pltpu.VMEM((R, pieces, K // pieces * H + 1, N, LANES), I16),
            pltpu.VMEM((NB, N, CB), F32),
            pltpu.VMEM((NB + 1, 2 * N, CB), BF16),
            pltpu.VMEM((K, N, CB), F32),
            pltpu.VMEM((R, 1, LANES), F32),
            pltpu.VMEM((2, C, 1, LANES), F32),
            pltpu.VMEM((slots + 1, N, CB), F32),
            pltpu.VMEM((NB, N, CB), F32),
            pltpu.VMEM((NB, N, CB), F32),
            pltpu.SMEM((S, B), jnp.int32),
            pltpu.SMEM((1, B), jnp.int32),
            pltpu.SMEM((slots,), jnp.int32),
            pltpu.VMEM((2, LANES), jnp.int32),
            pltpu.SMEM((2, LANES), jnp.int32),
            dma((B,)), dma((4,)),
            dma((2, C, Q)), dma((2, C, Q)),
            dma((R, pieces)), dma((R, pieces)), dma((R,)), dma((R,)),
            dma((R, pieces)), dma((R, pieces)), dma((2, C)), dma((2, C)),
        ],
        compiler_params=pltpu.CompilerParams(collective_id=0, has_side_effects=True),
    )(pattern.T, counts.T, right_side, tiles)
    smem = pl.BlockSpec(memory_space=pltpu.SMEM)
    return pl.pallas_call(
        closing,
        out_shape=(jax.ShapeDtypeStruct(x.shape, F32), jax.ShapeDtypeStruct((N,), F32)),
        in_specs=[vmem, smem],
        out_specs=(vmem, smem),
    )(x, mis)


def solution(mesh):
    R, C = mesh.shape["ray"], mesh.shape["cell"]
    in_specs = (P(None, "ray"), P("ray", "cell", None, None), P("ray", "cell"), P("ray", "cell"))
    out_specs = (P(None, "cell"), P())
    return jax.shard_map(
        functools.partial(local, R, C), mesh=mesh, in_specs=in_specs, out_specs=out_specs, check_vma=False
    )
```

```python
import functools

import jax
import jax.numpy as jnp
from jax import lax
from jax.experimental import pallas as pl
from jax.experimental.pallas import tpu as pltpu
from jax.sharding import PartitionSpec as P

BLK_DEV = 32
ITERS = 4
EPS = 1e-06
PIECES = 1
CUTS = 1
F32 = jnp.float32
BF16 = jnp.bfloat16
I16 = jnp.int16
LANES = 128
STEPS = 64.0
TOP = 32700.0


def split(value):
    hi = value.astype(BF16)
    lo = (value - hi.astype(F32)).astype(BF16)
    return hi, lo


def spread(stat, lanes):
    return jnp.concatenate([stat] * (lanes // LANES), axis=1)


def total_of(value):
    total = jnp.sum(value, axis=1, keepdims=True)
    return jnp.broadcast_to(total, (value.shape[0], LANES))


def diagonal(value, rows, axis):
    here = lax.broadcasted_iota(jnp.int32, (rows, LANES), 0) == lax.broadcasted_iota(jnp.int32, (rows, LANES), 1)
    return jnp.sum(jnp.where(here, value, 0.0), axis=axis, keepdims=True)


def to_row(stat):
    return diagonal(stat, stat.shape[0], 0)


def from_row(row, rows):
    return jnp.broadcast_to(diagonal(jnp.broadcast_to(row, (rows, LANES)), rows, 1), (rows, LANES))


def range_code(top):
    top = jnp.broadcast_to(jnp.max(top, axis=1, keepdims=True), (top.shape[0], LANES))
    return jnp.ceil(jnp.log2(jnp.maximum(top, 1e-30)) * STEPS) + 1.0


def put_code(message, code):
    message[message.shape[0] - 1] = code.astype(jnp.int32).astype(I16)


def put(message, k, value, code):
    parts = value.shape[1] // LANES
    scale = TOP * jnp.exp2(code * (-1.0 / STEPS))
    for j in range(parts):
        share = jnp.round(value[:, j * LANES:(j + 1) * LANES] * scale)
        message[k * parts + j] = share.astype(jnp.int32).astype(I16)


def unit(message, lanes):
    code = message[message.shape[0] - 1].astype(jnp.int32).astype(F32)
    return spread(jnp.exp2(code * (1.0 / STEPS)) * (1.0 / TOP), lanes)


def take(message, k, lanes):
    parts = lanes // LANES
    return jnp.concatenate([message[k * parts + j].astype(jnp.int32).astype(F32) for j in range(parts)], axis=1)


def flipped_bits(me, d):
    peer = me
    bit = 1
    while bit <= d:
        if d // bit % 2:
            peer = peer + bit - 2 * bit * lax.rem(me // bit, 2)
        bit *= 2
    return peer


def partners(me, n):
    if n & (n - 1) == 0:
        return [(d, flipped_bits(me, d)) for d in range(n - 1, 0, -1)]
    return [(d, lax.rem(me + d, n)) for d in range(1, n)]


def kernel(
    R, C,
    pattern_hbm, counts_hbm, rhs_hbm, tiles_hbm,
    out, mis,
    rhs, tiles, flipped, fpart, fq, u, ucat, aq, arecv, hq, vdec, vb, vsh, usq, gsq, cum, w, x,
    pattern, counts, idx, links_v, links,
    tile_sem, small_sem, fs, fr, as_, ar, ns, nr, hs, hr, gs, gr,
):
    S, B = pattern.shape
    N = rhs.shape[0]
    RB, CB = tiles.shape[2], tiles.shape[3]
    NB = BLK_DEV
    K = NB // R
    P, Q = aq.shape[1], fq.shape[2]
    KP, BQ = K // P, B // Q
    slots = B * S
    me_r = lax.axis_index("ray")
    me_c = lax.axis_index("cell")
    ray = partners(me_r, R)
    cell = partners(me_c, C)

    small = [
        pltpu.make_async_copy(pattern_hbm, pattern, small_sem.at[0]),
        pltpu.make_async_copy(counts_hbm, counts, small_sem.at[1]),
    ]
    seen = pltpu.make_async_copy(rhs_hbm, rhs, small_sem.at[3])
    for copy in small:
        copy.start()
    seen.start()
    loads = []
    for b in range(B):
        load = pltpu.make_async_copy(tiles_hbm.at[b], tiles.at[b], tile_sem.at[b])
        load.start()
        loads.append(load)

    barrier = pltpu.get_barrier_semaphore()
    for axis, others in (("cell", cell), ("ray", ray)):
        for _, peer in others:
            pl.semaphore_signal(barrier, inc=1, device_id={axis: peer}, device_id_type=pl.DeviceIdType.MESH)

    def remote(src, dst, send, recv, axis, peer):
        return pltpu.make_async_remote_copy(
            src_ref=src, dst_ref=dst, send_sem=send, recv_sem=recv,
            device_id={axis: peer}, device_id_type=pl.DeviceIdType.MESH,
        )

    cum[slots] = jnp.zeros((N, CB), F32)
    vb[NB] = jnp.zeros((2 * N, CB), BF16)
    w[...] = jnp.zeros_like(w)
    x[...] = jnp.zeros_like(x)
    vsh[...] = jnp.zeros_like(vsh)
    for copy in small:
        copy.wait()
    for b in range(B):
        for s in range(S):
            idx[b * S + s] = jnp.where(s < counts[0, b], pattern[s, b], NB)

    lane = lax.broadcasted_iota(jnp.int32, (8, LANES), 1)
    sub = lax.broadcasted_iota(jnp.int32, (8, LANES), 0)
    across = jnp.full((8, LANES), -1, jnp.int32)
    for i in range(slots):
        across = jnp.where(lane == i, idx[i], across)
    before = jnp.full((8, LANES), -1, jnp.int32)
    last = jnp.full((8, LANES), -1, jnp.int32)
    for j in range(0, slots, 8):
        down = jnp.full((8, LANES), -1, jnp.int32)
        for i in range(8):
            down = jnp.where(sub == i, idx[j + i], down)
        before = jnp.where((down == across) & (sub + j < lane), sub + j, before)
        last = jnp.where(down == lane, sub + j, last)
    before = jnp.max(before, axis=0, keepdims=True)
    last = jnp.max(last, axis=0, keepdims=True)
    links_v[0:1] = jnp.where(before < 0, slots, before)
    links_v[1:2] = jnp.where(last < 0, slots, last)
    table = pltpu.make_async_copy(links_v, links, small_sem.at[2])
    table.start()
    seen.wait()
    for b in range(B):
        value = rhs[:, b * RB:(b + 1) * RB]
        u[b] = value
        ucat[b] = value.astype(BF16)
    table.wait()

    def norm_copies():
        return [remote(usq.at[me_r], usq.at[me_r], ns.at[d], nr.at[d], "ray", peer) for d, peer in ray]

    def spread_copies(p):
        own = hq.at[me_r, p]
        return [remote(own, own, hs.at[d, p], hr.at[d, p], "ray", peer) for d, peer in ray]

    def scatter_copies(p):
        return [remote(aq.at[peer, p], arecv.at[d, p], as_.at[d, p], ar.at[d, p], "ray", peer) for d, peer in ray]

    def alpha_copies(side):
        own = gsq.at[side, me_c]
        return [remote(own, own, gs.at[side, d], gr.at[side, d], "cell", peer) for d, peer in cell]

    def time_copies(side, q):
        own = fq.at[side, me_c, q]
        return [remote(own, own, fs.at[side, d, q], fr.at[side, d, q], "cell", peer) for d, peer in cell]

    def start(copies):
        for copy in copies:
            copy.start()

    def finish(copies):
        for copy in copies:
            copy.wait()

    def norm_start():
        sq = jnp.zeros((N, RB), F32)
        for b in range(B):
            sq = sq + u[b] * u[b]
        return to_row(total_of(sq))

    def norm_send(total):
        usq[me_r] = total
        start(norm_copies())

    def norm_end():
        finish(norm_copies())
        total = usq[0]
        for r in range(1, R):
            total = total + usq[r]
        return jnp.sqrt(from_row(total, N) + EPS)

    def adjoint(wait, norm=None):
        for b in range(B):
            if wait:
                loads[b].wait()
            if norm is not None and b == B // 2:
                norm_send(norm)
            rows = ucat[b]
            for s in range(S):
                i = b * S + s
                per = lax.dot_general(rows, tiles[b, s], (((1,), (0,)), ((), ())), preferred_element_type=F32)
                cum[i] = per + cum[links[0, i]]
        top = jnp.zeros((N, CB), F32)
        for k in range(NB):
            top = jnp.maximum(top, jnp.abs(cum[links[1, k]]))
        code = range_code(top)
        for p in range(P):
            for r in range(R):
                for k in range(KP):
                    put(aq.at[r, p], k, cum[links[1, r * K + p * KP + k]], code)
                put_code(aq.at[r, p], code)

    def scatter_start():
        for p in range(P):
            start(scatter_copies(p))

    def gather(beta, alpha, beside):
        inv = spread(1.0 / beta, CB)
        back = spread(beta / alpha, CB)
        for p in range(P):
            for copy in scatter_copies(p):
                copy.wait_recv()
            units = {d: unit(arecv.at[d, p], CB) for d, _ in ray}
            top = jnp.zeros((N, CB), F32)
            for k in range(KP):
                total = cum[links[1, me_r * K + p * KP + k]]
                for d, _ in ray:
                    total = total + take(arecv.at[d, p], k, CB) * units[d]
                v = total * inv - back * vsh[p * KP + k]
                vsh[p * KP + k] = v
                top = jnp.maximum(top, jnp.abs(v))
            code = range_code(top)
            put_code(hq.at[me_r, p], code)
            for k in range(KP):
                put(hq.at[me_r, p], k, vsh[p * KP + k], code)
            start(spread_copies(p))
        for p in range(P):
            for copy in scatter_copies(p):
                copy.wait_send()
        beside()

    def forward(beta, side):
        sq = jnp.zeros((N, CB), F32)
        for p in range(P):
            finish(spread_copies(p))
            for r in range(R):
                grain = unit(hq.at[r, p], CB)
                for k in range(KP):
                    v = take(hq.at[r, p], k, CB) * grain
                    vdec[r * K + p * KP + k] = v
                    hi, lo = split(v)
                    vb[r * K + p * KP + k, 0:N] = hi
                    vb[r * K + p * KP + k, N:2 * N] = lo
                    sq = sq + v * v
        sq = to_row(total_of(sq))
        for q in range(Q):
            top = jnp.zeros((N, RB), F32)
            for b in range(q * BQ, (q + 1) * BQ):
                if b == B // 2:
                    gsq[side, me_c] = sq
                    start(alpha_copies(side))
                acc = jnp.zeros((2 * N, RB), F32)
                for s in range(S):
                    acc = acc + lax.dot_general(
                        vb[idx[b * S + s]], flipped[b, s], (((1,), (0,)), ((), ())), preferred_element_type=F32
                    )
                acc = acc[0:N] + acc[N:2 * N]
                fpart[b] = acc
                top = jnp.maximum(top, jnp.abs(acc))
            code = range_code(top)
            put_code(fq.at[side, me_c, q], code)
            for b in range(BQ):
                put(fq.at[side, me_c, q], b, fpart[q * BQ + b], code)
            start(time_copies(side, q))
        finish(alpha_copies(side))
        norm = gsq[side, 0]
        for j in range(1, C):
            norm = norm + gsq[side, j]
        alpha = jnp.sqrt(from_row(norm, N) + EPS)
        inv = spread(1.0 / alpha, RB)
        back = spread(alpha / beta, RB)
        for q in range(Q):
            finish(time_copies(side, q))
            units = [unit(fq.at[side, j, q], RB) for j in range(C)]
            for b in range(q * BQ, (q + 1) * BQ):
                total = take(fq.at[side, 0, q], b - q * BQ, RB) * units[0]
                for j in range(1, C):
                    total = total + take(fq.at[side, j, q], b - q * BQ, RB) * units[j]
                value = total * inv - back * u[b]
                u[b] = value
                ucat[b] = value.astype(BF16)
        return alpha

    def step_w(alpha, sine, rho):
        inv = spread(1.0 / alpha, CB)
        ratio = spread(sine * alpha / rho, CB)
        for k in range(NB):
            w[k] = vdec[k] * inv - ratio * w[k]

    def rotate(beta, rhobar, phibar):
        rho = jnp.sqrt(rhobar * rhobar + beta * beta)
        cosine = rhobar / rho
        sine = beta / rho
        phi = cosine * phibar
        return rho, cosine, sine, sine * phibar, phi / rho

    def flip():
        def one(i, carry):
            for s in range(S):
                flipped[i, s] = tiles[i, s].T
            return carry

        lax.fori_loop(0, B, one, 0)

    adjoint(True)
    pl.semaphore_wait(barrier, (C - 1) + (R - 1))
    norm_send(norm_start())
    scatter_start()
    flip()
    beta = norm_end()
    one = jnp.ones((N, LANES), F32)
    gather(beta, one, lambda: None)

    def body(step, carry):
        beta, cosine, sine, rho, phibar = carry
        alpha = forward(beta, lax.rem(step, 2))
        adjoint(False, norm_start())
        scatter_start()
        step_w(alpha, sine, rho)
        beta = norm_end()
        rho, cosine, sine, phibar, length = rotate(beta, -cosine * alpha, phibar)

        def step_x():
            scale = spread(length, CB)
            for k in range(NB):
                x[k] = x[k] + scale * w[k]

        gather(beta, alpha, step_x)
        return beta, cosine, sine, rho, phibar

    carry = (beta, -one, jnp.zeros((N, LANES), F32), one, beta)
    beta, cosine, sine, rho, phibar = lax.fori_loop(0, ITERS - 1, body, carry)
    alpha = forward(beta, (ITERS - 1) % 2)
    norm_send(norm_start())
    step_w(alpha, sine, rho)
    beta = norm_end()
    rho, cosine, sine, phibar, length = rotate(beta, -cosine * alpha, phibar)
    scale = spread(length, CB)
    for k in range(NB):
        out[:, k * CB:(k + 1) * CB] = x[k] + scale * w[k]
    mis[...] = phibar


def closing(x_ref, m_ref, out_ref, mis_ref):
    out_ref[...] = x_ref[...]
    for n in range(m_ref.shape[0]):
        mis_ref[n] = m_ref[n, 0]


def local(R, C, right_side, tiles, pattern, counts):
    N, rows = right_side.shape
    B, S, RB, CB = tiles.shape
    NB = BLK_DEV
    K = NB // R
    slots = B * S
    H = CB // LANES
    pieces = PIECES if K % PIECES == 0 else 1
    Q = CUTS if B % CUTS == 0 else 1
    assert RB == CB and NB % R == 0 and NB <= LANES and slots <= LANES and slots % 8 == 0
    vmem = pl.BlockSpec(memory_space=pltpu.VMEM)
    hbm = pl.BlockSpec(memory_space=pl.ANY)
    dma = pltpu.SemaphoreType.DMA
    x, mis = pl.pallas_call(
        functools.partial(kernel, R, C),
        out_shape=(
            jax.ShapeDtypeStruct((N, NB * CB), F32),
            jax.ShapeDtypeStruct((N, LANES), F32),
        ),
        in_specs=[hbm, hbm, hbm, hbm],
        out_specs=(vmem, vmem),
        scratch_shapes=[
            pltpu.VMEM((N, rows), F32),
            pltpu.VMEM((B, S, RB, CB), BF16),
            pltpu.VMEM((B, S, CB, RB), BF16),
            pltpu.VMEM((B, N, RB), F32),
            pltpu.VMEM((2, C, Q, B // Q * H + 1, N, LANES), I16),
            pltpu.VMEM((B, N, RB), F32),
            pltpu.VMEM((B, N, RB), BF16),
            pltpu.VMEM((R, pieces, K // pieces * H + 1, N, LANES), I16),
            pltpu.VMEM((R, pieces, K // pieces * H + 1, N, LANES), I16),
            pltpu.VMEM((R, pieces, K // pieces * H + 1, N, LANES), I16),
            pltpu.VMEM((NB, N, CB), F32),
            pltpu.VMEM((NB + 1, 2 * N, CB), BF16),
            pltpu.VMEM((K, N, CB), F32),
            pltpu.VMEM((R, 1, LANES), F32),
            pltpu.VMEM((2, C, 1, LANES), F32),
            pltpu.VMEM((slots + 1, N, CB), F32),
            pltpu.VMEM((NB, N, CB), F32),
            pltpu.VMEM((NB, N, CB), F32),
            pltpu.SMEM((S, B), jnp.int32),
            pltpu.SMEM((1, B), jnp.int32),
            pltpu.SMEM((slots,), jnp.int32),
            pltpu.VMEM((2, LANES), jnp.int32),
            pltpu.SMEM((2, LANES), jnp.int32),
            dma((B,)), dma((4,)),
            dma((2, C, Q)), dma((2, C, Q)),
            dma((R, pieces)), dma((R, pieces)), dma((R,)), dma((R,)),
            dma((R, pieces)), dma((R, pieces)), dma((2, C)), dma((2, C)),
        ],
        compiler_params=pltpu.CompilerParams(collective_id=0, has_side_effects=True),
    )(pattern.T, counts.T, right_side, tiles)
    smem = pl.BlockSpec(memory_space=pltpu.SMEM)
    return pl.pallas_call(
        closing,
        out_shape=(jax.ShapeDtypeStruct(x.shape, F32), jax.ShapeDtypeStruct((N,), F32)),
        in_specs=[vmem, smem],
        out_specs=(vmem, smem),
    )(x, mis)


def solution(mesh):
    R, C = mesh.shape["ray"], mesh.shape["cell"]
    in_specs = (P(None, "ray"), P("ray", "cell", None, None), P("ray", "cell"), P("ray", "cell"))
    out_specs = (P(None, "cell"), P())
    return jax.shard_map(
        functools.partial(local, R, C), mesh=mesh, in_specs=in_specs, out_specs=out_specs, check_vma=False
    )
```

```python
import functools

import jax
import jax.numpy as jnp
from jax import lax
from jax.experimental import pallas as pl
from jax.experimental.pallas import tpu as pltpu
from jax.sharding import PartitionSpec as P

BLK_DEV = 32
ITERS = 4
EPS = 1e-06
PIECES = 1
CUTS = 1
F32 = jnp.float32
BF16 = jnp.bfloat16
I16 = jnp.int16
LANES = 128
STEPS = 64.0
TOP = 32700.0


def split(value):
    hi = value.astype(BF16)
    lo = (value - hi.astype(F32)).astype(BF16)
    return hi, lo


def spread(stat, lanes):
    return jnp.concatenate([stat] * (lanes // LANES), axis=1)


def total_of(value):
    total = jnp.sum(value, axis=1, keepdims=True)
    return jnp.broadcast_to(total, (value.shape[0], LANES))


def diagonal(value, rows, axis):
    here = lax.broadcasted_iota(jnp.int32, (rows, LANES), 0) == lax.broadcasted_iota(jnp.int32, (rows, LANES), 1)
    return jnp.sum(jnp.where(here, value, 0.0), axis=axis, keepdims=True)


def to_row(stat):
    return diagonal(stat, stat.shape[0], 0)


def from_row(row, rows):
    return jnp.broadcast_to(diagonal(jnp.broadcast_to(row, (rows, LANES)), rows, 1), (rows, LANES))


def range_code(top):
    top = jnp.broadcast_to(jnp.max(top, axis=1, keepdims=True), (top.shape[0], LANES))
    return jnp.ceil(jnp.log2(jnp.maximum(top, 1e-30)) * STEPS) + 1.0


def put_code(message, code):
    message[message.shape[0] - 1] = code.astype(jnp.int32).astype(I16)


def put(message, k, value, code):
    parts = value.shape[1] // LANES
    scale = TOP * jnp.exp2(code * (-1.0 / STEPS))
    for j in range(parts):
        share = jnp.round(value[:, j * LANES:(j + 1) * LANES] * scale)
        message[k * parts + j] = share.astype(jnp.int32).astype(I16)


def unit(message, lanes):
    code = message[message.shape[0] - 1].astype(jnp.int32).astype(F32)
    return spread(jnp.exp2(code * (1.0 / STEPS)) * (1.0 / TOP), lanes)


def take(message, k, lanes):
    parts = lanes // LANES
    return jnp.concatenate([message[k * parts + j].astype(jnp.int32).astype(F32) for j in range(parts)], axis=1)


def flipped_bits(me, d):
    peer = me
    bit = 1
    while bit <= d:
        if d // bit % 2:
            peer = peer + bit - 2 * bit * lax.rem(me // bit, 2)
        bit *= 2
    return peer


def partners(me, n):
    if n & (n - 1) == 0:
        return [(d, flipped_bits(me, d)) for d in range(n - 1, 0, -1)]
    return [(d, lax.rem(me + d, n)) for d in range(1, n)]


def kernel(
    R, C,
    pattern_hbm, counts_hbm, rhs_hbm, tiles_hbm,
    out, mis,
    rhs, tiles, flipped, fpart, fq, u, ucat, aq, arecv, hq, vdec, vb, vsh, usq, gsq, cum, w, x,
    pattern, counts, idx, links_v, links,
    tile_sem, small_sem, fs, fr, as_, ar, ns, nr, hs, hr, gs, gr,
):
    S, B = pattern.shape
    N = rhs.shape[0]
    RB, CB = tiles.shape[2], tiles.shape[3]
    NB = BLK_DEV
    K = NB // R
    P, Q = aq.shape[1], fq.shape[2]
    KP, BQ = K // P, B // Q
    slots = B * S
    me_r = lax.axis_index("ray")
    me_c = lax.axis_index("cell")
    ray = partners(me_r, R)
    cell = partners(me_c, C)

    small = [
        pltpu.make_async_copy(pattern_hbm, pattern, small_sem.at[0]),
        pltpu.make_async_copy(counts_hbm, counts, small_sem.at[1]),
    ]
    seen = pltpu.make_async_copy(rhs_hbm, rhs, small_sem.at[3])
    for copy in small:
        copy.start()
    seen.start()
    loads = []
    for b in range(B):
        load = pltpu.make_async_copy(tiles_hbm.at[b], tiles.at[b], tile_sem.at[b])
        load.start()
        loads.append(load)

    barrier = pltpu.get_barrier_semaphore()
    for axis, others in (("cell", cell), ("ray", ray)):
        for _, peer in others:
            pl.semaphore_signal(barrier, inc=1, device_id={axis: peer}, device_id_type=pl.DeviceIdType.MESH)

    def remote(src, dst, send, recv, axis, peer):
        return pltpu.make_async_remote_copy(
            src_ref=src, dst_ref=dst, send_sem=send, recv_sem=recv,
            device_id={axis: peer}, device_id_type=pl.DeviceIdType.MESH,
        )

    cum[slots] = jnp.zeros((N, CB), F32)
    vb[NB] = jnp.zeros((2 * N, CB), BF16)
    w[...] = jnp.zeros_like(w)
    x[...] = jnp.zeros_like(x)
    vsh[...] = jnp.zeros_like(vsh)
    for copy in small:
        copy.wait()
    for b in range(B):
        for s in range(S):
            idx[b * S + s] = jnp.where(s < counts[0, b], pattern[s, b], NB)

    lane = lax.broadcasted_iota(jnp.int32, (8, LANES), 1)
    sub = lax.broadcasted_iota(jnp.int32, (8, LANES), 0)
    across = jnp.full((8, LANES), -1, jnp.int32)
    for i in range(slots):
        across = jnp.where(lane == i, idx[i], across)
    before = jnp.full((8, LANES), -1, jnp.int32)
    last = jnp.full((8, LANES), -1, jnp.int32)
    for j in range(0, slots, 8):
        down = jnp.full((8, LANES), -1, jnp.int32)
        for i in range(8):
            down = jnp.where(sub == i, idx[j + i], down)
        before = jnp.where((down == across) & (sub + j < lane), sub + j, before)
        last = jnp.where(down == lane, sub + j, last)
    before = jnp.max(before, axis=0, keepdims=True)
    last = jnp.max(last, axis=0, keepdims=True)
    links_v[0:1] = jnp.where(before < 0, slots, before)
    links_v[1:2] = jnp.where(last < 0, slots, last)
    table = pltpu.make_async_copy(links_v, links, small_sem.at[2])
    table.start()
    seen.wait()
    for b in range(B):
        value = rhs[:, b * RB:(b + 1) * RB]
        u[b] = value
        hi, lo = split(value)
        ucat[b, 0:N] = hi
        ucat[b, N:2 * N] = lo
    table.wait()

    def norm_copies():
        return [remote(usq.at[me_r], usq.at[me_r], ns.at[d], nr.at[d], "ray", peer) for d, peer in ray]

    def spread_copies(p):
        own = hq.at[me_r, p]
        return [remote(own, own, hs.at[d, p], hr.at[d, p], "ray", peer) for d, peer in ray]

    def scatter_copies(p):
        return [remote(aq.at[d, p], arecv.at[d, p], as_.at[d, p], ar.at[d, p], "ray", peer) for d, peer in ray]

    def alpha_copies(side):
        own = gsq.at[side, me_c]
        return [remote(own, own, gs.at[side, d], gr.at[side, d], "cell", peer) for d, peer in cell]

    def time_copies(side, q):
        own = fq.at[side, me_c, q]
        return [remote(own, own, fs.at[side, d, q], fr.at[side, d, q], "cell", peer) for d, peer in cell]

    def start(copies):
        for copy in copies:
            copy.start()

    def finish(copies):
        for copy in copies:
            copy.wait()

    def norm_start():
        sq = jnp.zeros((N, RB), F32)
        for b in range(B):
            sq = sq + u[b] * u[b]
        return to_row(total_of(sq))

    def norm_send(total):
        usq[me_r] = total
        start(norm_copies())

    def norm_end():
        finish(norm_copies())
        total = usq[0]
        for r in range(1, R):
            total = total + usq[r]
        return jnp.sqrt(from_row(total, N) + EPS)

    def adjoint(wait, norm=None):
        for b in range(B):
            if wait:
                loads[b].wait()
            if norm is not None and b == B // 2:
                norm_send(norm)
            rows = ucat[b]
            for s in range(S):
                i = b * S + s
                per = lax.dot_general(rows, tiles[b, s], (((1,), (0,)), ((), ())), preferred_element_type=F32)
                cum[i] = per[0:N] + per[N:2 * N] + cum[links[0, i]]
        top = jnp.zeros((N, CB), F32)
        for k in range(NB):
            top = jnp.maximum(top, jnp.abs(cum[links[1, k]]))
        code = range_code(top)
        return code

    def scatter_start(code):
        for p in range(P):
            for (d, peer), copy in zip(ray, scatter_copies(p)):
                put_code(aq.at[d, p], code)
                for k in range(KP):
                    put(aq.at[d, p], k, cum[links[1, peer * K + p * KP + k]], code)
                copy.start()

    def gather(beta, alpha, beside):
        inv = spread(1.0 / beta, CB)
        back = spread(beta / alpha, CB)
        for p in range(P):
            for copy in scatter_copies(p):
                copy.wait_recv()
            units = {d: unit(arecv.at[d, p], CB) for d, _ in ray}
            top = jnp.zeros((N, CB), F32)
            for k in range(KP):
                total = cum[links[1, me_r * K + p * KP + k]]
                for d, _ in ray:
                    total = total + take(arecv.at[d, p], k, CB) * units[d]
                v = total * inv - back * vsh[p * KP + k]
                vsh[p * KP + k] = v
                top = jnp.maximum(top, jnp.abs(v))
            code = range_code(top)
            put_code(hq.at[me_r, p], code)
            for k in range(KP):
                put(hq.at[me_r, p], k, vsh[p * KP + k], code)
            start(spread_copies(p))
        for p in range(P):
            for copy in scatter_copies(p):
                copy.wait_send()
        beside()

    def forward(beta, side):
        sq = jnp.zeros((N, CB), F32)
        for p in range(P):
            finish(spread_copies(p))
            for r in range(R):
                grain = unit(hq.at[r, p], CB)
                for k in range(KP):
                    v = take(hq.at[r, p], k, CB) * grain
                    vdec[r * K + p * KP + k] = v
                    hi, lo = split(v)
                    vb[r * K + p * KP + k, 0:N] = hi
                    vb[r * K + p * KP + k, N:2 * N] = lo
                    sq = sq + v * v
        sq = to_row(total_of(sq))
        for q in range(Q):
            top = jnp.zeros((N, RB), F32)
            for b in range(q * BQ, (q + 1) * BQ):
                if b == B // 2:
                    gsq[side, me_c] = sq
                    start(alpha_copies(side))
                acc = jnp.zeros((2 * N, RB), F32)
                for s in range(S):
                    acc = acc + lax.dot_general(
                        vb[idx[b * S + s]], flipped[b, s], (((1,), (0,)), ((), ())), preferred_element_type=F32
                    )
                acc = acc[0:N] + acc[N:2 * N]
                fpart[b] = acc
                top = jnp.maximum(top, jnp.abs(acc))
            code = range_code(top)
            put_code(fq.at[side, me_c, q], code)
            for b in range(BQ):
                put(fq.at[side, me_c, q], b, fpart[q * BQ + b], code)
            start(time_copies(side, q))
        finish(alpha_copies(side))
        norm = gsq[side, 0]
        for j in range(1, C):
            norm = norm + gsq[side, j]
        alpha = jnp.sqrt(from_row(norm, N) + EPS)
        inv = spread(1.0 / alpha, RB)
        back = spread(alpha / beta, RB)
        for q in range(Q):
            finish(time_copies(side, q))
            units = [unit(fq.at[side, j, q], RB) for j in range(C)]
            for b in range(q * BQ, (q + 1) * BQ):
                total = take(fq.at[side, 0, q], b - q * BQ, RB) * units[0]
                for j in range(1, C):
                    total = total + take(fq.at[side, j, q], b - q * BQ, RB) * units[j]
                value = total * inv - back * u[b]
                u[b] = value
                hi, lo = split(value)
                ucat[b, 0:N] = hi
                ucat[b, N:2 * N] = lo
        return alpha

    def step_w(alpha, sine, rho):
        inv = spread(1.0 / alpha, CB)
        ratio = spread(sine * alpha / rho, CB)
        for k in range(NB):
            w[k] = vdec[k] * inv - ratio * w[k]

    def rotate(beta, rhobar, phibar):
        rho = jnp.sqrt(rhobar * rhobar + beta * beta)
        cosine = rhobar / rho
        sine = beta / rho
        phi = cosine * phibar
        return rho, cosine, sine, sine * phibar, phi / rho

    def flip():
        def one(i, carry):
            for s in range(S):
                flipped[i, s] = tiles[i, s].T
            return carry

        lax.fori_loop(0, B, one, 0)

    code = adjoint(True)
    pl.semaphore_wait(barrier, (C - 1) + (R - 1))
    norm_send(norm_start())
    scatter_start(code)
    flip()
    beta = norm_end()
    one = jnp.ones((N, LANES), F32)
    gather(beta, one, lambda: None)

    def body(step, carry):
        beta, cosine, sine, rho, phibar = carry
        alpha = forward(beta, lax.rem(step, 2))
        scatter_start(adjoint(False, norm_start()))
        step_w(alpha, sine, rho)
        beta = norm_end()
        rho, cosine, sine, phibar, length = rotate(beta, -cosine * alpha, phibar)

        def step_x():
            scale = spread(length, CB)
            for k in range(NB):
                x[k] = x[k] + scale * w[k]

        gather(beta, alpha, step_x)
        return beta, cosine, sine, rho, phibar

    carry = (beta, -one, jnp.zeros((N, LANES), F32), one, beta)
    beta, cosine, sine, rho, phibar = lax.fori_loop(0, ITERS - 1, body, carry)
    alpha = forward(beta, (ITERS - 1) % 2)
    norm_send(norm_start())
    step_w(alpha, sine, rho)
    beta = norm_end()
    rho, cosine, sine, phibar, length = rotate(beta, -cosine * alpha, phibar)
    scale = spread(length, CB)
    for k in range(NB):
        out[:, k * CB:(k + 1) * CB] = x[k] + scale * w[k]
    mis[...] = phibar


def closing(x_ref, m_ref, out_ref, mis_ref):
    out_ref[...] = x_ref[...]
    for n in range(m_ref.shape[0]):
        mis_ref[n] = m_ref[n, 0]


def local(R, C, right_side, tiles, pattern, counts):
    N, rows = right_side.shape
    B, S, RB, CB = tiles.shape
    NB = BLK_DEV
    K = NB // R
    slots = B * S
    H = CB // LANES
    pieces = PIECES if K % PIECES == 0 else 1
    Q = CUTS if B % CUTS == 0 else 1
    assert RB == CB and NB % R == 0 and NB <= LANES and slots <= LANES and slots % 8 == 0
    vmem = pl.BlockSpec(memory_space=pltpu.VMEM)
    hbm = pl.BlockSpec(memory_space=pl.ANY)
    dma = pltpu.SemaphoreType.DMA
    x, mis = pl.pallas_call(
        functools.partial(kernel, R, C),
        out_shape=(
            jax.ShapeDtypeStruct((N, NB * CB), F32),
            jax.ShapeDtypeStruct((N, LANES), F32),
        ),
        in_specs=[hbm, hbm, hbm, hbm],
        out_specs=(vmem, vmem),
        scratch_shapes=[
            pltpu.VMEM((N, rows), F32),
            pltpu.VMEM((B, S, RB, CB), BF16),
            pltpu.VMEM((B, S, CB, RB), BF16),
            pltpu.VMEM((B, N, RB), F32),
            pltpu.VMEM((2, C, Q, B // Q * H + 1, N, LANES), I16),
            pltpu.VMEM((B, N, RB), F32),
            pltpu.VMEM((B, 2 * N, RB), BF16),
            pltpu.VMEM((R, pieces, K // pieces * H + 1, N, LANES), I16),
            pltpu.VMEM((R, pieces, K // pieces * H + 1, N, LANES), I16),
            pltpu.VMEM((R, pieces, K // pieces * H + 1, N, LANES), I16),
            pltpu.VMEM((NB, N, CB), F32),
            pltpu.VMEM((NB + 1, 2 * N, CB), BF16),
            pltpu.VMEM((K, N, CB), F32),
            pltpu.VMEM((R, 1, LANES), F32),
            pltpu.VMEM((2, C, 1, LANES), F32),
            pltpu.VMEM((slots + 1, N, CB), F32),
            pltpu.VMEM((NB, N, CB), F32),
            pltpu.VMEM((NB, N, CB), F32),
            pltpu.SMEM((S, B), jnp.int32),
            pltpu.SMEM((1, B), jnp.int32),
            pltpu.SMEM((slots,), jnp.int32),
            pltpu.VMEM((2, LANES), jnp.int32),
            pltpu.SMEM((2, LANES), jnp.int32),
            dma((B,)), dma((4,)),
            dma((2, C, Q)), dma((2, C, Q)),
            dma((R, pieces)), dma((R, pieces)), dma((R,)), dma((R,)),
            dma((R, pieces)), dma((R, pieces)), dma((2, C)), dma((2, C)),
        ],
        compiler_params=pltpu.CompilerParams(collective_id=0, has_side_effects=True),
    )(pattern.T, counts.T, right_side, tiles)
    smem = pl.BlockSpec(memory_space=pltpu.SMEM)
    return pl.pallas_call(
        closing,
        out_shape=(jax.ShapeDtypeStruct(x.shape, F32), jax.ShapeDtypeStruct((N,), F32)),
        in_specs=[vmem, smem],
        out_specs=(vmem, smem),
    )(x, mis)


def solution(mesh):
    R, C = mesh.shape["ray"], mesh.shape["cell"]
    in_specs = (P(None, "ray"), P("ray", "cell", None, None), P("ray", "cell"), P("ray", "cell"))
    out_specs = (P(None, "cell"), P())
    return jax.shard_map(
        functools.partial(local, R, C), mesh=mesh, in_specs=in_specs, out_specs=out_specs, check_vma=False
    )
```
